32 devices in a mesh: row: 8 (over z, x), col: 4 (over y, core).
Axes of the slice: x: 2, y: 2, z: 4, core: 2. Of those that a mesh axis runs over, the one named last changes fastest.
Arguments:
- object_slices: float32 [2, 4, 2048, 1024], P(None, None, 'row', 'col'), may hold values from -1 to 1
- positions: int32 [8, 4, 2, 2], P('row', 'col'), may hold values from 0 to 128
- intensities: float32 [8, 4, 2, 256, 256], P('row', 'col'), may hold values from 0 to 0.8
- probe: float32 [2, 256, 256], replicated, may hold values from -6 to 6
- propagator: float32 [256, 256], replicated, may hold values from -3.140625 to 3.140625
Outputs:
- gradient: float32 [2, 4, 2048, 1024], P(None, None, 'row', 'col')
- updated: float32 [2, 4, 2048, 1024], P(None, None, 'row', 'col')
The draws below stay inside these ranges and needn't reach their ends.
Inputs may be any that keep to these rules, and one draw needn't show every extreme that they name: `positions`: each probe window lies inside its tile widened by 64 pixels on every side.
All inputs are finite; a program needn't handle non-finite values.
Results may differ from the reference program's by a relative error of at most 0.0003.
Values sent between devices are 32-bit elements; how exact they have to be, the bound alone decides.
A program may use at most 128 MiB of HBM per device.

```python
import jax
import jax.numpy as jnp
from jax import lax

CORE = 256
HALO = 64
W = 256
SLICES = 4
PROBES = 2
NY = 2048
NX = 1024
N_ROW = 8
N_COL = 4


def plant(entries, rng, smallest, high):
    shape = entries.shape
    place = [jax.random.randint(jax.random.fold_in(rng, axis), (), 0, shape[axis]) for axis in range(len(shape))]
    entries = entries.at[tuple(place)].set(smallest)
    longest = shape.index(max(shape))
    place[longest] = (place[longest] + 1) % shape[longest]
    return entries.at[tuple(place)].set(high)


def block_scale(stream_key, dims, split, low, top_value):
    gain, own = 1.0, jax.random.fold_in(stream_key, 6)
    for axis_at, shards_of in split:
        heights = jnp.exp(jax.random.uniform(jax.random.fold_in(own, axis_at), (shards_of,), jnp.float32, low / len(split), top_value / len(split)))
        gain = gain * jnp.repeat(heights, dims[axis_at] // shards_of).reshape([-1 if axis == axis_at else 1 for axis in range(len(dims))])
    return gain


def bell_draw(rng, extent, scale, limit, held_as=jnp.bfloat16):
    array = jax.random.normal(rng, extent, jnp.float32) * scale
    return jnp.minimum(jnp.maximum(array, -limit), limit).astype(held_as)


def setup_inputs(seed: int = 0) -> dict:
    splits = jax.random.split(jax.random.key(seed), 6)
    object_slices = jnp.clip(jax.random.uniform(splits[0], (2, SLICES, NY, NX), jnp.float32, -1.0, 1.0) * block_scale(splits[0], (2, SLICES, NY, NX), ((2, 8), (3, 4)), -0.4, 0.0), -1.0, 1.0)
    positions = plant(jax.random.randint(splits[1], (N_ROW, N_COL, PROBES, 2), 0, CORE + 2 * HALO - W + 1), jax.random.fold_in(splits[1], 1), 0, CORE + 2 * HALO - W).astype(jnp.int32)
    intensities = jnp.clip(0.8 * jax.random.uniform(splits[2], (N_ROW, N_COL, PROBES, W, W), jnp.float32) ** block_scale(splits[2], (N_ROW, N_COL, PROBES, W, W), ((0, 8), (1, 4)), -0.2, 0.2), 0.0, 0.8)
    probe = bell_draw(splits[3], (2, W, W), 1.0, 6.0, jnp.float32)
    propagator = jnp.clip(jax.random.uniform(splits[4], (W, W), jnp.float32, -3.140625, 3.140625), -3.140625, 3.140625)
    return {"object_slices": object_slices, "positions": positions, "intensities": intensities, "probe": probe, "propagator": propagator}


descent_rate = 0.5

def tables(width):
    counter = jnp.arange(width, dtype=jnp.int32)
    product = counter[:, None] * counter[None, :] % width
    angles = product.astype(jnp.float32) * (2.0 * jnp.pi / width)
    norming = 1.0 / jnp.sqrt(jnp.float32(width))
    return (jnp.cos(angles) * norming, jnp.sin(angles) * norming)

def apply_left(matrix, field):
    return jnp.einsum('ab,kbc->kac', matrix, field, precision=lax.Precision.HIGHEST)

def apply_right(field, matrix):
    return jnp.einsum('kab,bc->kac', field, matrix, precision=lax.Precision.HIGHEST)

def fourier(real_part, imag_part, cosines, sines, direction):
    half_re = apply_left(cosines, real_part) - direction * apply_left(sines, imag_part)
    half_im = apply_left(cosines, imag_part) + direction * apply_left(sines, real_part)
    full_re = apply_right(half_re, cosines) - direction * apply_right(half_im, sines)
    full_im = apply_right(half_im, cosines) + direction * apply_right(half_re, sines)
    return (full_re, full_im)

def complex_product(left_re, left_im, right_re, right_im):
    return (left_re * right_re - left_im * right_im, left_re * right_im + left_im * right_re)

def probe_gradients(windows, probe, propagator, measured):
    width = probe.shape[-1]
    layers = windows.shape[2]
    count = windows.shape[0]
    cosines, sines = tables(width)
    phase_re = jnp.cos(propagator)
    phase_im = jnp.sin(propagator)
    wave_re = jnp.broadcast_to(probe[0], (count, width, width))
    wave_im = jnp.broadcast_to(probe[1], (count, width, width))
    stored = []
    for layer in range(layers):
        stored.append((wave_re, wave_im))
        exit_re, exit_im = complex_product(wave_re, wave_im, windows[:, 0, layer], windows[:, 1, layer])
        if layer < layers - 1:
            freq_re, freq_im = fourier(exit_re, exit_im, cosines, sines, -1.0)
            freq_re, freq_im = complex_product(freq_re, freq_im, phase_re, phase_im)
            wave_re, wave_im = fourier(freq_re, freq_im, cosines, sines, 1.0)
    far_re, far_im = fourier(exit_re, exit_im, cosines, sines, -1.0)
    misfit = far_re * far_re + far_im * far_im - measured
    back_re, back_im = fourier(misfit * far_re, misfit * far_im, cosines, sines, 1.0)
    real_terms = [None] * layers
    imag_terms = [None] * layers
    for layer in range(layers - 1, -1, -1):
        wave_re, wave_im = stored[layer]
        real_terms[layer] = wave_re * back_re + wave_im * back_im
        imag_terms[layer] = wave_re * back_im - wave_im * back_re
        if layer > 0:
            slab_re = windows[:, 0, layer]
            slab_im = windows[:, 1, layer]
            back_re, back_im = (slab_re * back_re + slab_im * back_im, slab_re * back_im - slab_im * back_re)
            freq_re, freq_im = fourier(back_re, back_im, cosines, sines, -1.0)
            freq_re, freq_im = complex_product(freq_re, freq_im, phase_re, -phase_im)
            back_re, back_im = fourier(freq_re, freq_im, cosines, sines, 1.0)
    real_stack = jnp.stack(real_terms, axis=1)
    imag_stack = jnp.stack(imag_terms, axis=1)
    return jnp.stack([real_stack, imag_stack], axis=1)

def reference(object_slices, positions, intensities, probe, propagator):
    total_rows = object_slices.shape[2]
    total_cols = object_slices.shape[3]
    width = probe.shape[-1]
    counter = jnp.arange(width, dtype=jnp.int32)

    def cut_window(row_index, col_index):
        return object_slices[:, :, row_index][:, :, :, col_index]

    def one_tile(gradient_sum, tile_index):
        tile_row = tile_index // N_COL
        tile_col = tile_index % N_COL
        offsets = positions[tile_row, tile_col]
        row_start = tile_row * CORE - HALO + offsets[:, 0]
        col_start = tile_col * CORE - HALO + offsets[:, 1]
        row_index = ((row_start[:, None] + counter[None, :]) % total_rows).astype(jnp.int32)
        col_index = ((col_start[:, None] + counter[None, :]) % total_cols).astype(jnp.int32)
        windows = jax.vmap(cut_window)(row_index, col_index)
        terms = probe_gradients(windows, probe, propagator, intensities[tile_row, tile_col])

        def add_one(index, running):
            return running.at[:, :, row_index[index][:, None], col_index[index][None, :]].add(terms[index])
        gradient_sum = lax.fori_loop(0, terms.shape[0], add_one, gradient_sum)
        return (gradient_sum, None)
    zeros = jnp.zeros_like(object_slices)
    gradient, _ = lax.scan(one_tile, zeros, jnp.arange(N_ROW * N_COL, dtype=jnp.int32))
    return (gradient, object_slices - descent_rate * gradient)
```

```python
import functools

import jax
import jax.numpy as jnp
import numpy as np
from jax import lax
from jax.experimental import pallas as pl
from jax.experimental.pallas import tpu as pltpu
from jax.sharding import PartitionSpec as P

HALO = 64
LANES = 128

descent_rate = 0.5


def split(value):
    high = value.astype(jnp.bfloat16)
    low = (value - high.astype(jnp.float32)).astype(jnp.bfloat16)
    return high, low


def half_tables(width):
    half = width // 2
    place = np.arange(half)
    found = []
    for odd in (0, 1):
        angle = 2.0 * np.pi * (np.outer(2 * place + odd, place) % width) / width
        re = np.cos(angle) / np.sqrt(width)
        im = -np.sin(angle) / np.sqrt(width)
        found.append(np.block([[re, -im], [im, re]]).astype(np.float32))
    even, odd = found
    order = np.eye(width, dtype=np.float32)[np.concatenate([2 * place, 2 * place + 1])]
    six = np.stack([even, odd, even.T, odd.T, order, order.T])
    high = six.astype(jnp.bfloat16)
    low = (six - high.astype(np.float32)).astype(jnp.bfloat16)
    return np.stack([high, low])


def dot_left(pair, value):
    high, low = split(value)
    matrix = jnp.concatenate([pair[0], pair[0], pair[1]], 1)
    return jnp.dot(matrix, jnp.concatenate([high, low, high], 0), preferred_element_type=jnp.float32)


def dot_right(value, pair):
    high, low = split(value)
    matrix = jnp.concatenate([pair[0], pair[0], pair[1]], 0)
    return jnp.dot(jnp.concatenate([high, low, high], 1), matrix, preferred_element_type=jnp.float32)


def cut(value, dim):
    half = value.shape[dim] // 2
    return (lax.slice_in_dim(value, 0, half, axis=dim), lax.slice_in_dim(value, half, 2 * half, axis=dim))


def joined(first, second, dim):
    return jnp.concatenate([first, second], dim)


def forward_axis(re, im, dim, dot, even_matrix, odd_matrix):
    r0, r1 = cut(re, dim)
    i0, i1 = cut(im, dim)
    even_re, even_im = cut(dot(joined(r0 + r1, i0 + i1, dim), even_matrix), dim)
    odd_re, odd_im = cut(dot(joined(r0 - r1, i0 - i1, dim), odd_matrix), dim)
    return joined(even_re, odd_re, dim), joined(even_im, odd_im, dim)


def inverse_axis(re, im, dim, dot, even_matrix, odd_matrix):
    r0, r1 = cut(re, dim)
    i0, i1 = cut(im, dim)
    p_re, p_im = cut(dot(joined(r0, i0, dim), even_matrix), dim)
    q_re, q_im = cut(dot(joined(r1, i1, dim), odd_matrix), dim)
    return joined(p_re + q_re, p_re - q_re, dim), joined(p_im + q_im, p_im - q_im, dim)


def left_dot(value, pair):
    return dot_left(pair, value)


def turned_over(value, width, source, target):
    parts = [lax.slice_in_dim(value, at, at + width, axis=source) for at in range(0, value.shape[source], width)]
    return jnp.concatenate(parts, target)


def forward(re, im, pairs):
    width = re.shape[0]
    re, im = forward_axis(re, im, 0, left_dot, pairs(0), pairs(1))
    re, im = (turned_over(v, width, 1, 0) for v in (re, im))
    return forward_axis(re, im, 1, dot_right, pairs(2), pairs(3))


def inverse(re, im, pairs):
    width = re.shape[1]
    re, im = inverse_axis(re, im, 1, dot_right, pairs(0), pairs(1))
    re, im = (turned_over(v, width, 0, 1) for v in (re, im))
    return inverse_axis(re, im, 0, left_dot, pairs(2), pairs(3))


def hop(fields, phase_re, phase_im, pairs):
    width = fields[0][0].shape[0]
    re, im = forward(*(jnp.concatenate([f[c] for f in fields], 1) for c in range(2)), pairs)
    re, im = complex_product(re, im, *(jnp.concatenate([p] * len(fields), 0) for p in (phase_re, phase_im)))
    re, im = inverse(re, im, pairs)
    spans = [slice(at, at + width) for at in range(0, re.shape[1], width)]
    return [(re[:, span], im[:, span]) for span in spans]


def by_parity(value, left, right):
    rows = jnp.dot(
        jnp.concatenate([left, left], 1), jnp.concatenate(split(value), 0), preferred_element_type=jnp.float32
    )
    return jnp.dot(
        jnp.concatenate(split(rows), 1), jnp.concatenate([right, right], 0), preferred_element_type=jnp.float32
    )


def complex_product(left_re, left_im, right_re, right_im):
    return (left_re * right_re - left_im * right_im, left_re * right_im + left_im * right_re)


def slid(whole, shift, axis, span):
    turned = pltpu.roll(whole, lax.rem(span - shift, span), axis)
    kept = lax.broadcasted_iota(jnp.int32, whole[:-1].shape, axis) < span - shift
    return jnp.where(kept, turned[:-1], turned[1:])


def spread(whole, shift, axis, span):
    turned = pltpu.roll(whole, lax.rem(shift, span), axis)
    zero = jnp.zeros_like(turned[:1])
    first = jnp.concatenate([zero, turned], 0)
    other = jnp.concatenate([turned, zero], 0)
    moved = lax.broadcasted_iota(jnp.int32, first.shape, axis) < shift
    return jnp.where(moved, first, other)


def row_place(oy, rows, width):
    base = jnp.minimum(lax.div(oy, 8), (rows - width) // 8 - 1)
    return base, oy - 8 * base


def lane_place(ox):
    early = ox < HALO
    return jnp.where(early, 2, 0), jnp.where(early, ox + LANES - HALO, ox - HALO)


def swapped(value):
    return pltpu.roll(value, HALO, value.ndim - 1)


def choose(low, high):
    lower = lax.broadcasted_iota(jnp.int32, low.shape, low.ndim - 1) < HALO
    return jnp.where(lower, low, high)


def ends_of(cells):
    (re0, re1), (im0, im1) = cells
    return choose(re0, swapped(im0)), choose(swapped(re1), im1)


def middle_of(cells):
    return [choose(swapped(first), swapped(second)) for first, second in cells]


def unpacked(head, tail, middle_re, middle_im):
    mid_re, mid_im = swapped(middle_re), swapped(middle_im)
    return (
        (choose(head, mid_re), choose(mid_re, swapped(tail))),
        (choose(swapped(head), mid_im), choose(mid_im, tail)),
    )


def step_kernel(
    offsets, objects, intensities, probe, propagator, tables_in,
    gradient, updated,
    tables, cells, measured, ordered, phase, phases, waves, windows, slab, spans, total,
    row_out, row_in, col_out, col_in, corner_in,
    grow_out, grow_in, gcol_out, gcol_in, gcorner_out, gcorner_in,
    load_sem, slice_sem, store_sem, row_sem, col_sem, corner_sem, grow_sem, gcol_sem, gcorner_sem,
):
    count, width = measured.shape[0], measured.shape[-1]
    layers, tall = cells.shape[1:3]
    last = layers - 1
    wide = cells.shape[3] // LANES
    rounds = wide + 1
    whole = tall + 2 * HALO
    pad = 2 * HALO

    rows_n, cols_n = lax.axis_size("row"), lax.axis_size("col")
    row, col = lax.axis_index("row"), lax.axis_index("col")
    below, above = lax.rem(row + 1, rows_n), lax.rem(row + rows_n - 1, rows_n)
    right, left = lax.rem(col + 1, cols_n), lax.rem(col + cols_n - 1, cols_n)
    row_to = ((below, col), (above, col))
    col_to = ((row, right), (row, left))

    def send(src, dst, sems, where, target):
        return pltpu.make_async_remote_copy(
            src_ref=src, dst_ref=dst, send_sem=sems.at[(0, *where)], recv_sem=sems.at[(1, *where)],
            device_id=target, device_id_type=pl.DeviceIdType.MESH,
        )

    def row_copy(layer, half, d):
        where = (layer, half, slice(None), d)
        return send(row_out.at[where], row_in.at[where], row_sem, (layer, half, d), row_to[d])

    def col_copy(layer, side):
        return send(col_out.at[layer, side], col_in.at[layer, side], col_sem, (layer, side), col_to[side])

    def corner_copy(layer, side):
        source = row_in.at[layer, 0, 1 - side]
        return send(source, corner_in.at[layer, side], corner_sem, (layer, side), col_to[side])

    def grow_copy(layer, half, d):
        where = (layer, half, slice(None), d)
        return send(grow_out.at[where], grow_in.at[where], grow_sem, (layer, half, d), row_to[d])

    def gcol_copy(layer, side):
        return send(gcol_out.at[layer, side], gcol_in.at[layer, side], gcol_sem, (layer, side), col_to[side])

    def gcorner_copy(layer, side):
        return send(
            gcorner_out.at[layer, side], gcorner_in.at[layer, side], gcorner_sem, (layer, side), col_to[side]
        )

    loads = [
        pltpu.make_async_copy(propagator, phase, load_sem.at[0]),
        pltpu.make_async_copy(tables_in, tables, load_sem.at[1]),
        pltpu.make_async_copy(intensities, measured, load_sem.at[2]),
    ] + [pltpu.make_async_copy(probe, waves.at[k, 0], load_sem.at[3 + k]) for k in range(count)]

    def slice_load(layer):
        return pltpu.make_async_copy(objects.at[:, layer], cells.at[:, layer], slice_sem.at[layer])

    barrier = pltpu.get_barrier_semaphore()
    for target in row_to + col_to:
        pl.semaphore_signal(barrier, inc=1, device_id=target, device_id_type=pl.DeviceIdType.MESH)
    for layer in range(layers):
        slice_load(layer).start()
    for load in loads:
        load.start()

    def lane_blocks(ref, layer, rows):
        return [[ref[c, layer, rows, pl.ds(j * LANES, LANES)] for j in range(wide)] for c in range(2)]

    def pack(layer, carry):
        slice_load(layer).wait()
        for d, at in enumerate((tall - HALO, 0)):
            strip = lane_blocks(cells, layer, pl.ds(at, HALO))
            for half, packs in enumerate((ends_of(strip), middle_of(strip))):
                for i in range(2):
                    row_out[layer, half, i, d] = packs[i]
        head, tail = ends_of(lane_blocks(cells, layer, pl.ds(0, tall)))
        col_out[layer, 0] = tail
        col_out[layer, 1] = head
        return carry

    lax.fori_loop(0, layers, pack, 0)
    pl.semaphore_wait(barrier, 4)

    def launch(layer, carry):
        for half in range(2):
            for d in range(2):
                row_copy(layer, half, d).start()
        for side in range(2):
            col_copy(layer, side).start()
        return carry

    lax.fori_loop(0, layers, launch, 0)

    def pairs(index):
        return tables[0, index], tables[1, index]

    for load in loads:
        load.wait()
    angle = phase[...]
    phases[0] = by_parity(jnp.cos(angle), tables[0, 4], tables[0, 5])
    phases[1] = by_parity(jnp.sin(angle), tables[0, 4], tables[0, 5])
    for k in range(count):
        ordered[k] = by_parity(measured[k], tables[0, 4], tables[0, 5])
    blank = jnp.zeros((pad // 8, 8, LANES), jnp.float32)
    for k in range(count):
        for c in range(2):
            for j in range(rounds):
                spans[k, c, j, pl.ds(0, pad // 8)] = blank
                spans[k, c, j, pl.ds((pad + width) // 8 + 1, pad // 8)] = blank

    pieces = ((0, HALO, 0), (HALO, tall, None), (HALO + tall, HALO, 1))

    def forward_corners(layer):
        for d in range(2):
            row_copy(layer, 0, d).wait_recv()
        for side in range(2):
            corner_copy(layer, side).start()

    def assemble(layer):
        for d in range(2):
            row_copy(layer, 1, d).wait_recv()
        for side in range(2):
            col_copy(layer, side).wait_recv()
            corner_copy(layer, side).wait_recv()
        for start, size, d in pieces:
            rows, tiles = pl.ds(start // 8, size // 8), (size // 8, 8, LANES)
            if d is None:
                blocks = lane_blocks(cells, layer, pl.ds(0, tall))
                l, r = col_in[layer, 0], col_in[layer, 1]
            else:
                blocks = unpacked(*(row_in[layer, half, i, d] for half in range(2) for i in range(2)))
                l, r = corner_in[layer, 0, d], corner_in[layer, 1, d]
            for c in range(2):
                for j in range(wide):
                    slab[c, j, rows] = blocks[c][j].reshape(tiles)
            slab[0, wide, rows] = choose(r, swapped(l)).reshape(tiles)
            slab[1, wide, rows] = choose(swapped(r), l).reshape(tiles)

    def cut_layer(k, layer):
        base, shift = row_place(offsets[0, 0, k, 0], whole, width)
        first, turn = lane_place(offsets[0, 0, k, 1])
        for c in range(2):
            blocks = jnp.stack(
                [slab[c, lax.rem(first + j, rounds), pl.ds(base, width // 8 + 1)] for j in range(rounds)]
            )
            blocks = slid(blocks, turn, 3, LANES)
            for j in range(wide):
                part = slid(blocks[j], shift, 1, 8)
                windows[k, layer, c, :, j * LANES : j * LANES + LANES] = part.reshape(width, LANES)

    def leave(k, layer):
        return complex_product(
            waves[k, layer, 0], waves[k, layer, 1], windows[k, layer, 0], windows[k, layer, 1]
        )

    def onward(layer, carry):
        forward_corners(layer)
        assemble(layer)
        for k in range(count):
            cut_layer(k, layer)
        fields = [leave(k, layer) for k in range(count)]
        for k, (re, im) in enumerate(hop(fields, phases[0], phases[1], pairs)):
            waves[k, layer + 1, 0] = re
            waves[k, layer + 1, 1] = im
        return carry

    lax.fori_loop(0, last, onward, 0)

    def record(k, layer, back_re, back_im):
        wave_re, wave_im = waves[k, layer, 0], waves[k, layer, 1]
        shift = row_place(offsets[0, 0, k, 0], whole, width)[1]
        turn = lane_place(offsets[0, 0, k, 1])[1]
        terms = (wave_re * back_re + wave_im * back_im, wave_re * back_im - wave_im * back_re)
        for c in range(2):
            blocks = jnp.stack([terms[c][:, j * LANES : j * LANES + LANES] for j in range(wide)])
            blocks = spread(blocks, turn, 2, LANES)
            for j in range(rounds):
                part = spread(blocks[j].reshape(width // 8, 8, LANES), shift, 1, 8)
                spans[k, c, j, pl.ds(pad // 8, width // 8 + 1)] = part

    def summed(c, block, start, size):
        found = None
        for k in range(count):
            base = row_place(offsets[0, 0, k, 0], whole, width)[0]
            first = lane_place(offsets[0, 0, k, 1])[0]
            at = (pad + start) // 8 - base
            term = spans[k, c, lax.rem(block + rounds - first, rounds), pl.ds(at, size // 8)]
            found = term if found is None else found + term
        return found.reshape(size, LANES)

    def settle(layer):
        for start, size, d in pieces:
            blocks = [[summed(c, j, start, size) for j in range(wide)] for c in range(2)]
            outer_re, outer_im = (summed(c, wide, start, size) for c in range(2))
            to_right, to_left = choose(outer_re, swapped(outer_im)), choose(swapped(outer_re), outer_im)
            if d is None:
                for c in range(2):
                    for j in range(wide):
                        total[c, layer, :, j * LANES : j * LANES + LANES] = blocks[c][j]
                gcol_out[layer, 0] = to_right
                gcol_out[layer, 1] = to_left
            else:
                for half, packs in enumerate((ends_of(blocks), middle_of(blocks))):
                    for i in range(2):
                        grow_out[layer, half, i, 1 - d] = packs[i]
                gcorner_out[layer, 0, 1 - d] = to_right
                gcorner_out[layer, 1, 1 - d] = to_left
        for side in range(2):
            gcorner_copy(layer, side).start()
        for d in range(2):
            grow_copy(layer, 1, d).start()
        for side in range(2):
            gcol_copy(layer, side).start()

    def pass_on(layer):
        for side in range(2):
            gcorner_copy(layer, side).wait_recv()
        for d in range(2):
            for side in range(2):
                grow_out[layer, 0, side, d] += gcorner_in[layer, side, d]
            grow_copy(layer, 0, d).start()

    forward_corners(last)
    assemble(last)
    for k in range(count):
        cut_layer(k, last)
    for k in range(count):
        far_re, far_im = forward(*leave(k, last), pairs)
        misfit = far_re * far_re + far_im * far_im - ordered[k]
        back_re, back_im = inverse(misfit * far_re, misfit * far_im, pairs)
        record(k, last, back_re, back_im)
        waves[k, last, 0] = back_re
        waves[k, last, 1] = back_im
    settle(last)

    def backward(step, carry):
        layer = last - step
        fields = []
        for k in range(count):
            back_re, back_im = waves[k, layer, 0], waves[k, layer, 1]
            slab_re, slab_im = windows[k, layer, 0], windows[k, layer, 1]
            fields.append(complex_product(back_re, back_im, slab_re, -slab_im))
        backs = hop(fields, phases[0], -phases[1], pairs)
        pass_on(layer)
        for k, (re, im) in enumerate(backs):
            record(k, layer - 1, re, im)
            waves[k, layer - 1, 0] = re
            waves[k, layer - 1, 1] = im
        settle(layer - 1)
        return carry

    lax.fori_loop(0, last, backward, 0)
    pass_on(0)

    def stores(layer):
        return (
            pltpu.make_async_copy(total.at[:, layer], gradient.at[:, layer], store_sem.at[0, layer]),
            pltpu.make_async_copy(cells.at[:, layer], updated.at[:, layer], store_sem.at[1, layer]),
        )

    def finish(step, carry):
        layer = last - step
        for side in range(2):
            gcol_copy(layer, side).wait_recv()
        for half in (1, 0):
            for d in range(2):
                grow_copy(layer, half, d).wait_recv()
        spots = ((0, HALO, 0), (HALO, tall - 2 * HALO, None), (tall - HALO, HALO, 1))
        for start, size, d in spots:
            rows = pl.ds(start, size)
            sums = lane_blocks(total, layer, rows)
            if d is not None:
                added = unpacked(*(grow_in[layer, half, i, d] for half in range(2) for i in range(2)))
                sums = [[sums[c][j] + added[c][j] for j in range(wide)] for c in range(2)]
            l, r = gcol_in[layer, 0, rows, :], gcol_in[layer, 1, rows, :]
            zero = jnp.zeros_like(l)
            sums[0][0] += choose(l, zero)
            sums[1][0] += choose(swapped(l), zero)
            sums[0][wide - 1] += choose(zero, swapped(r))
            sums[1][wide - 1] += choose(zero, r)
            for c in range(2):
                for j in range(wide):
                    lanes = pl.ds(j * LANES, LANES)
                    total[c, layer, rows, lanes] = sums[c][j]
                    cells[c, layer, rows, lanes] -= descent_rate * sums[c][j]
        for store in stores(layer):
            store.start()
        return carry

    lax.fori_loop(0, layers, finish, 0)

    def close(layer, carry):
        for d in range(2):
            for half in range(2):
                row_copy(layer, half, d).wait_send()
                grow_copy(layer, half, d).wait_send()
            col_copy(layer, d).wait_send()
            corner_copy(layer, d).wait_send()
            gcol_copy(layer, d).wait_send()
            gcorner_copy(layer, d).wait_send()
        for store in stores(layer):
            store.wait()
        return carry

    lax.fori_loop(0, layers, close, 0)


def on_device(object_slices, positions, intensities, probe, propagator):
    count, width = intensities.shape[2], intensities.shape[-1]
    layers, tall, broad = object_slices.shape[1:]
    rounds = broad // LANES + 1
    tables = jnp.asarray(half_tables(width))
    anywhere = pl.BlockSpec(memory_space=pl.ANY)
    like = jax.ShapeDtypeStruct(object_slices.shape, object_slices.dtype)
    f32 = functools.partial(pltpu.VMEM, dtype=jnp.float32)
    strip, side, corner = (layers, 2, 2, 2, HALO, LANES), (layers, 2, tall, LANES), (layers, 2, 2, HALO, LANES)
    dma = pltpu.SemaphoreType.DMA
    return tuple(
        pl.pallas_call(
            step_kernel,
            out_shape=[like, like],
            in_specs=[pl.BlockSpec(memory_space=pltpu.SMEM)] + [anywhere] * 5,
            out_specs=[anywhere] * 2,
            scratch_shapes=[
                pltpu.VMEM(tables.shape, tables.dtype),
                f32(object_slices.shape),
                f32((count, width, width)),
                f32((count, width, width)),
                f32((width, width)),
                f32((2, width, width)),
                f32((count, layers, 2, width, width)),
                f32((count, layers, 2, width, width)),
                f32((2, rounds, (tall + 2 * HALO) // 8, 8, LANES)),
                f32((count, 2, rounds, (width + 4 * HALO) // 8 + 1, 8, LANES)),
                f32(object_slices.shape),
                f32(strip), f32(strip), f32(side), f32(side), f32(corner),
                f32(strip), f32(strip), f32(side), f32(side), f32(corner), f32(corner),
                dma((3 + count,)), dma((layers,)), dma((2, layers)),
                dma((2, layers, 2, 2)), dma((2, layers, 2)), dma((2, layers, 2)),
                dma((2, layers, 2, 2)), dma((2, layers, 2)), dma((2, layers, 2)),
            ],
            compiler_params=pltpu.CompilerParams(
                collective_id=0, has_side_effects=True, vmem_limit_bytes=58 * 2**20
            ),
        )(positions, object_slices, intensities.reshape(count, width, width), probe, propagator, tables)
    )


def solution(mesh):
    return jax.shard_map(
        on_device,
        mesh=mesh,
        in_specs=(
            P(None, None, "row", "col"),
            P("row", "col", None, None),
            P("row", "col", None, None, None),
            P(),
            P(),
        ),
        out_specs=(P(None, None, "row", "col"), P(None, None, "row", "col")),
        check_vma=False,
    )
```

```python
import functools

import jax
import jax.numpy as jnp
import numpy as np
from jax import lax
from jax.experimental import pallas as pl
from jax.experimental.pallas import tpu as pltpu
from jax.sharding import PartitionSpec as P

HALO = 64
LANES = 128

descent_rate = 0.5


def split(value):
    high = value.astype(jnp.bfloat16)
    low = (value - high.astype(jnp.float32)).astype(jnp.bfloat16)
    return high, low


def half_tables(width):
    half = width // 2
    place = np.arange(half)
    found = []
    for odd in (0, 1):
        angle = 2.0 * np.pi * (np.outer(2 * place + odd, place) % width) / width
        re = np.cos(angle) / np.sqrt(width)
        im = -np.sin(angle) / np.sqrt(width)
        found.append(np.block([[re, -im], [im, re]]).astype(np.float32))
    even, odd = found
    order = np.eye(width, dtype=np.float32)[np.concatenate([2 * place, 2 * place + 1])]
    six = np.stack([even, odd, even.T, odd.T, order, order.T])
    high = six.astype(jnp.bfloat16)
    low = (six - high.astype(np.float32)).astype(jnp.bfloat16)
    return np.stack([high, low])


def dot_left(pair, value):
    high, low = split(value)
    matrix = jnp.concatenate([pair[0], pair[0], pair[1]], 1)
    return jnp.dot(matrix, jnp.concatenate([high, low, high], 0), preferred_element_type=jnp.float32)


def dot_right(value, pair):
    high, low = split(value)
    matrix = jnp.concatenate([pair[0], pair[0], pair[1]], 0)
    return jnp.dot(jnp.concatenate([high, low, high], 1), matrix, preferred_element_type=jnp.float32)


def cut(value, dim):
    half = value.shape[dim] // 2
    return (lax.slice_in_dim(value, 0, half, axis=dim), lax.slice_in_dim(value, half, 2 * half, axis=dim))


def joined(first, second, dim):
    return jnp.concatenate([first, second], dim)


def forward_axis(re, im, dim, dot, even_matrix, odd_matrix):
    r0, r1 = cut(re, dim)
    i0, i1 = cut(im, dim)
    even_re, even_im = cut(dot(joined(r0 + r1, i0 + i1, dim), even_matrix), dim)
    odd_re, odd_im = cut(dot(joined(r0 - r1, i0 - i1, dim), odd_matrix), dim)
    return joined(even_re, odd_re, dim), joined(even_im, odd_im, dim)


def inverse_axis(re, im, dim, dot, even_matrix, odd_matrix):
    r0, r1 = cut(re, dim)
    i0, i1 = cut(im, dim)
    p_re, p_im = cut(dot(joined(r0, i0, dim), even_matrix), dim)
    q_re, q_im = cut(dot(joined(r1, i1, dim), odd_matrix), dim)
    return joined(p_re + q_re, p_re - q_re, dim), joined(p_im + q_im, p_im - q_im, dim)


def left_dot(value, pair):
    return dot_left(pair, value)


def turned_over(value, width, source, target):
    parts = [lax.slice_in_dim(value, at, at + width, axis=source) for at in range(0, value.shape[source], width)]
    return jnp.concatenate(parts, target)


def forward(re, im, pairs):
    width = re.shape[0]
    re, im = forward_axis(re, im, 0, left_dot, pairs(0), pairs(1))
    re, im = (turned_over(v, width, 1, 0) for v in (re, im))
    return forward_axis(re, im, 1, dot_right, pairs(2), pairs(3))


def inverse(re, im, pairs):
    width = re.shape[1]
    re, im = inverse_axis(re, im, 1, dot_right, pairs(0), pairs(1))
    re, im = (turned_over(v, width, 0, 1) for v in (re, im))
    return inverse_axis(re, im, 0, left_dot, pairs(2), pairs(3))


def hop(fields, phase_re, phase_im, pairs):
    width = fields[0][0].shape[0]
    re, im = forward(*(jnp.concatenate([f[c] for f in fields], 1) for c in range(2)), pairs)
    re, im = complex_product(re, im, *(jnp.concatenate([p] * len(fields), 0) for p in (phase_re, phase_im)))
    re, im = inverse(re, im, pairs)
    spans = [slice(at, at + width) for at in range(0, re.shape[1], width)]
    return [(re[:, span], im[:, span]) for span in spans]


def by_parity(value, left, right):
    rows = jnp.dot(
        jnp.concatenate([left, left], 1), jnp.concatenate(split(value), 0), preferred_element_type=jnp.float32
    )
    return jnp.dot(
        jnp.concatenate(split(rows), 1), jnp.concatenate([right, right], 0), preferred_element_type=jnp.float32
    )


def complex_product(left_re, left_im, right_re, right_im):
    return (left_re * right_re - left_im * right_im, left_re * right_im + left_im * right_re)


def slid(whole, shift, axis, span):
    turned = pltpu.roll(whole, lax.rem(span - shift, span), axis)
    kept = lax.broadcasted_iota(jnp.int32, whole[:-1].shape, axis) < span - shift
    return jnp.where(kept, turned[:-1], turned[1:])


def spread(whole, shift, axis, span):
    turned = pltpu.roll(whole, lax.rem(shift, span), axis)
    zero = jnp.zeros_like(turned[:1])
    first = jnp.concatenate([zero, turned], 0)
    other = jnp.concatenate([turned, zero], 0)
    moved = lax.broadcasted_iota(jnp.int32, first.shape, axis) < shift
    return jnp.where(moved, first, other)


def row_place(oy, rows, width):
    base = jnp.minimum(lax.div(oy, 8), (rows - width) // 8 - 1)
    return base, oy - 8 * base


def lane_place(ox):
    early = ox < HALO
    return jnp.where(early, 2, 0), jnp.where(early, ox + LANES - HALO, ox - HALO)


def swapped(value):
    return pltpu.roll(value, HALO, value.ndim - 1)


def choose(low, high):
    lower = lax.broadcasted_iota(jnp.int32, low.shape, low.ndim - 1) < HALO
    return jnp.where(lower, low, high)


def ends_of(cells):
    (re0, re1), (im0, im1) = cells
    return choose(re0, swapped(im0)), choose(swapped(re1), im1)


def middle_of(cells):
    return [choose(swapped(first), swapped(second)) for first, second in cells]


def unpacked(head, tail, middle_re, middle_im):
    mid_re, mid_im = swapped(middle_re), swapped(middle_im)
    return (
        (choose(head, mid_re), choose(mid_re, swapped(tail))),
        (choose(swapped(head), mid_im), choose(mid_im, tail)),
    )


def step_kernel(
    offsets_in, objects, intensities, probe, propagator, tables_in,
    gradient, updated,
    offsets, tables, cells, measured, ordered, phase, phases, waves, windows, slab, spans,
    row_out, row_in, col_out, col_in, corner_in,
    grow_out, grow_in, gcol_out, gcol_in, gcorner_out, gcorner_in,
    load_sem, slice_sem, row_sem, col_sem, corner_sem, grow_sem, gcol_sem, gcorner_sem,
):
    count, width = measured.shape[0], measured.shape[-1]
    layers, tall = cells.shape[1:3]
    last = layers - 1
    wide = cells.shape[3] // LANES
    rounds = wide + 1
    whole = tall + 2 * HALO
    pad = 2 * HALO

    rows_n, cols_n = lax.axis_size("row"), lax.axis_size("col")
    row, col = lax.axis_index("row"), lax.axis_index("col")
    below, above = lax.rem(row + 1, rows_n), lax.rem(row + rows_n - 1, rows_n)
    right, left = lax.rem(col + 1, cols_n), lax.rem(col + cols_n - 1, cols_n)
    row_to = ((below, col), (above, col))
    soon = lax.rem(lax.div(row + 1, 2), 2)
    col_to = ((row, right), (row, left))

    def send(src, dst, sems, where, target):
        return pltpu.make_async_remote_copy(
            src_ref=src, dst_ref=dst, send_sem=sems.at[(0, *where)], recv_sem=sems.at[(1, *where)],
            device_id=target, device_id_type=pl.DeviceIdType.MESH,
        )

    def row_copy(layer, half, d):
        where = (layer, half, slice(None), d)
        target = (lax.rem(row + rows_n + 1 - 2 * d, rows_n), col)
        return send(row_out.at[where], row_in.at[where], row_sem, (layer, half, d), target)

    def col_copy(layer, side):
        return send(col_out.at[layer, side], col_in.at[layer, side], col_sem, (layer, side), col_to[side])

    def corner_copy(layer, side):
        source = row_in.at[layer, 0, 1 - side]
        return send(source, corner_in.at[layer, side], corner_sem, (layer, side), col_to[side])

    def grow_copy(layer, half, d):
        where = (layer, half, slice(None), d)
        return send(grow_out.at[where], grow_in.at[where], grow_sem, (layer, half, d), row_to[d])

    def gcol_copy(layer, side):
        return send(gcol_out.at[layer, side], gcol_in.at[layer, side], gcol_sem, (layer, side), col_to[side])

    def gcorner_copy(layer, side):
        return send(
            gcorner_out.at[layer, side], gcorner_in.at[layer, side], gcorner_sem, (layer, side), col_to[side]
        )

    loads = [
        pltpu.make_async_copy(propagator, phase, load_sem.at[0]),
        pltpu.make_async_copy(tables_in, tables, load_sem.at[1]),
        pltpu.make_async_copy(intensities, measured, load_sem.at[2]),
        pltpu.make_async_copy(offsets_in, offsets, load_sem.at[3]),
    ] + [pltpu.make_async_copy(probe, waves.at[k, 0], load_sem.at[4 + k]) for k in range(count)]

    def slice_load(layer):
        return pltpu.make_async_copy(objects.at[:, layer], cells.at[:, layer], slice_sem.at[layer])

    barrier = pltpu.get_barrier_semaphore()
    for target in row_to + col_to:
        pl.semaphore_signal(barrier, inc=1, device_id=target, device_id_type=pl.DeviceIdType.MESH)
    for layer in range(layers):
        slice_load(layer).start()

    def lane_blocks(ref, layer, rows):
        return [[ref[c, layer, rows, pl.ds(j * LANES, LANES)] for j in range(wide)] for c in range(2)]

    def pack(layer):
        slice_load(layer).wait()
        for d, at in enumerate((tall - HALO, 0)):
            strip = lane_blocks(cells, layer, pl.ds(at, HALO))
            for half, packs in enumerate((ends_of(strip), middle_of(strip))):
                for i in range(2):
                    row_out[layer, half, i, d] = packs[i]
        head, tail = ends_of(lane_blocks(cells, layer, pl.ds(0, tall)))
        col_out[layer, 0] = tail
        col_out[layer, 1] = head

    def launch(layer):
        for half in range(2):
            row_copy(layer, half, soon).start()
        for side in range(2):
            col_copy(layer, side).start()

    def pack_and_launch(layer, carry):
        pack(layer)
        launch(layer)
        return carry

    def launch_late(layer, carry):
        for half in range(2):
            row_copy(layer, half, 1 - soon).start()
        return carry

    pack(0)
    pl.semaphore_wait(barrier, 4)
    launch(0)
    for load in loads:
        load.start()
    lax.fori_loop(1, layers, pack_and_launch, 0)
    lax.fori_loop(0, layers, launch_late, 0)

    def pairs(index):
        return tables[0, index], tables[1, index]

    for load in loads:
        load.wait()
    angle = phase[...]
    phases[0] = by_parity(jnp.cos(angle), tables[0, 4], tables[0, 5])
    phases[1] = by_parity(jnp.sin(angle), tables[0, 4], tables[0, 5])
    for k in range(count):
        ordered[k] = by_parity(measured[k], tables[0, 4], tables[0, 5])
    blank = jnp.zeros((pad // 8, 8, LANES), jnp.float32)
    for k in range(count):
        for c in range(2):
            for j in range(rounds):
                spans[k, c, j, pl.ds(0, pad // 8)] = blank
                spans[k, c, j, pl.ds((pad + width) // 8 + 1, pad // 8)] = blank

    pieces = ((0, HALO, 0), (HALO, tall, None), (HALO + tall, HALO, 1))

    def forward_corners(layer):
        for d in range(2):
            row_copy(layer, 0, d).wait_recv()
        for side in range(2):
            corner_copy(layer, side).start()

    def assemble(layer):
        for d in range(2):
            row_copy(layer, 1, d).wait_recv()
        for side in range(2):
            col_copy(layer, side).wait_recv()
            corner_copy(layer, side).wait_recv()
        for start, size, d in pieces:
            rows, tiles = pl.ds(start // 8, size // 8), (size // 8, 8, LANES)
            if d is None:
                blocks = lane_blocks(cells, layer, pl.ds(0, tall))
                l, r = col_in[layer, 0], col_in[layer, 1]
            else:
                blocks = unpacked(*(row_in[layer, half, i, d] for half in range(2) for i in range(2)))
                l, r = corner_in[layer, 0, d], corner_in[layer, 1, d]
            for c in range(2):
                for j in range(wide):
                    slab[c, j, rows] = blocks[c][j].reshape(tiles)
            slab[0, wide, rows] = choose(r, swapped(l)).reshape(tiles)
            slab[1, wide, rows] = choose(swapped(r), l).reshape(tiles)

    def cut_layer(k, layer):
        base, shift = row_place(offsets[0, 0, k, 0], whole, width)
        first, turn = lane_place(offsets[0, 0, k, 1])
        for c in range(2):
            blocks = jnp.stack(
                [slab[c, lax.rem(first + j, rounds), pl.ds(base, width // 8 + 1)] for j in range(rounds)]
            )
            blocks = slid(blocks, turn, 3, LANES)
            for j in range(wide):
                part = slid(blocks[j], shift, 1, 8)
                windows[k, layer, c, :, j * LANES : j * LANES + LANES] = part.reshape(width, LANES)

    def leave(k, layer):
        return complex_product(
            waves[k, layer, 0], waves[k, layer, 1], windows[k, layer, 0], windows[k, layer, 1]
        )

    def onward(layer, carry):
        assemble(layer)
        for k in range(count):
            cut_layer(k, layer)
        forward_corners(layer + 1)
        fields = [leave(k, layer) for k in range(count)]
        for k, (re, im) in enumerate(hop(fields, phases[0], phases[1], pairs)):
            waves[k, layer + 1, 0] = re
            waves[k, layer + 1, 1] = im
        return carry

    forward_corners(0)
    lax.fori_loop(0, last, onward, 0)

    def record(k, layer, back_re, back_im):
        wave_re, wave_im = waves[k, layer, 0], waves[k, layer, 1]
        shift = row_place(offsets[0, 0, k, 0], whole, width)[1]
        turn = lane_place(offsets[0, 0, k, 1])[1]
        terms = (wave_re * back_re + wave_im * back_im, wave_re * back_im - wave_im * back_re)
        for c in range(2):
            blocks = jnp.stack([terms[c][:, j * LANES : j * LANES + LANES] for j in range(wide)])
            blocks = spread(blocks, turn, 2, LANES)
            for j in range(rounds):
                part = spread(blocks[j].reshape(width // 8, 8, LANES), shift, 1, 8)
                spans[k, c, j, pl.ds(pad // 8, width // 8 + 1)] = part

    def summed(c, block, start, size):
        found = None
        for k in range(count):
            base = row_place(offsets[0, 0, k, 0], whole, width)[0]
            first = lane_place(offsets[0, 0, k, 1])[0]
            at = (pad + start) // 8 - base
            term = spans[k, c, lax.rem(block + rounds - first, rounds), pl.ds(at, size // 8)]
            found = term if found is None else found + term
        return found.reshape(size, LANES)

    def settle(layer):
        for start, size, d in pieces:
            blocks = [[summed(c, j, start, size) for j in range(wide)] for c in range(2)]
            outer_re, outer_im = (summed(c, wide, start, size) for c in range(2))
            to_right, to_left = choose(outer_re, swapped(outer_im)), choose(swapped(outer_re), outer_im)
            if d is None:
                for c in range(2):
                    for j in range(wide):
                        gradient[c, layer, :, j * LANES : j * LANES + LANES] = blocks[c][j]
                gcol_out[layer, 0] = to_right
                gcol_out[layer, 1] = to_left
            else:
                for half, packs in enumerate((ends_of(blocks), middle_of(blocks))):
                    for i in range(2):
                        grow_out[layer, half, i, 1 - d] = packs[i]
                gcorner_out[layer, 0, 1 - d] = to_right
                gcorner_out[layer, 1, 1 - d] = to_left
        for side in range(2):
            gcorner_copy(layer, side).start()
        for d in range(2):
            grow_copy(layer, 1, d).start()
        for side in range(2):
            gcol_copy(layer, side).start()

    def pass_on(layer):
        for side in range(2):
            gcorner_copy(layer, side).wait_recv()
        for d in range(2):
            for side in range(2):
                grow_out[layer, 0, side, d] += gcorner_in[layer, side, d]
            grow_copy(layer, 0, d).start()

    assemble(last)
    for k in range(count):
        cut_layer(k, last)
    for k in range(count):
        far_re, far_im = forward(*leave(k, last), pairs)
        misfit = far_re * far_re + far_im * far_im - ordered[k]
        back_re, back_im = inverse(misfit * far_re, misfit * far_im, pairs)
        record(k, last, back_re, back_im)
        waves[k, last, 0] = back_re
        waves[k, last, 1] = back_im
    settle(last)

    def backward(step, carry):
        layer = last - step
        fields = []
        for k in range(count):
            back_re, back_im = waves[k, layer, 0], waves[k, layer, 1]
            slab_re, slab_im = windows[k, layer, 0], windows[k, layer, 1]
            fields.append(complex_product(back_re, back_im, slab_re, -slab_im))
        backs = hop(fields, phases[0], -phases[1], pairs)
        pass_on(layer)
        for k, (re, im) in enumerate(backs):
            record(k, layer - 1, re, im)
            waves[k, layer - 1, 0] = re
            waves[k, layer - 1, 1] = im
        settle(layer - 1)
        return carry

    lax.fori_loop(0, last, backward, 0)
    pass_on(0)

    def finish(step, carry):
        layer = last - step
        for side in range(2):
            gcol_copy(layer, side).wait_recv()
        for half in (1, 0):
            for d in range(2):
                grow_copy(layer, half, d).wait_recv()
        spots = ((0, HALO, 0), (HALO, tall - 2 * HALO, None), (tall - HALO, HALO, 1))
        for start, size, d in spots:
            rows = pl.ds(start, size)
            sums = lane_blocks(gradient, layer, rows)
            if d is not None:
                added = unpacked(*(grow_in[layer, half, i, d] for half in range(2) for i in range(2)))
                sums = [[sums[c][j] + added[c][j] for j in range(wide)] for c in range(2)]
            l, r = gcol_in[layer, 0, rows, :], gcol_in[layer, 1, rows, :]
            zero = jnp.zeros_like(l)
            sums[0][0] += choose(l, zero)
            sums[1][0] += choose(swapped(l), zero)
            sums[0][wide - 1] += choose(zero, swapped(r))
            sums[1][wide - 1] += choose(zero, r)
            for c in range(2):
                for j in range(wide):
                    lanes = pl.ds(j * LANES, LANES)
                    gradient[c, layer, rows, lanes] = sums[c][j]
                    updated[c, layer, rows, lanes] = cells[c, layer, rows, lanes] - descent_rate * sums[c][j]
        return carry

    lax.fori_loop(0, layers, finish, 0)

    def close(layer, carry):
        for d in range(2):
            for half in range(2):
                row_copy(layer, half, d).wait_send()
                grow_copy(layer, half, d).wait_send()
            col_copy(layer, d).wait_send()
            corner_copy(layer, d).wait_send()
            gcol_copy(layer, d).wait_send()
            gcorner_copy(layer, d).wait_send()
        return carry

    lax.fori_loop(0, layers, close, 0)


def publish_kernel(gradient, updated, gradient_out, updated_out, sems):
    copies = (
        pltpu.make_async_copy(gradient, gradient_out, sems.at[0]),
        pltpu.make_async_copy(updated, updated_out, sems.at[1]),
    )
    for copy in copies:
        copy.start()
    for copy in copies:
        copy.wait()


def on_device(object_slices, positions, intensities, probe, propagator):
    count, width = intensities.shape[2], intensities.shape[-1]
    layers, tall, broad = object_slices.shape[1:]
    rounds = broad // LANES + 1
    tables = jnp.asarray(half_tables(width))
    anywhere = pl.BlockSpec(memory_space=pl.ANY)
    f32 = functools.partial(pltpu.VMEM, dtype=jnp.float32)
    strip, side, corner = (layers, 2, 2, 2, HALO, LANES), (layers, 2, tall, LANES), (layers, 2, 2, HALO, LANES)
    dma = pltpu.SemaphoreType.DMA
    held = pltpu.VMEM(object_slices.shape, object_slices.dtype)
    pair = [held, held]
    found = pl.pallas_call(
        step_kernel,
        out_shape=pair,
        in_specs=[anywhere] * 6,
        out_specs=[pl.BlockSpec(memory_space=pltpu.VMEM)] * 2,
        scratch_shapes=[
            pltpu.SMEM(positions.shape, positions.dtype),
            pltpu.VMEM(tables.shape, tables.dtype),
            f32(object_slices.shape),
            f32((count, width, width)),
            f32((count, width, width)),
            f32((width, width)),
            f32((2, width, width)),
            f32((count, layers, 2, width, width)),
            f32((count, layers, 2, width, width)),
            f32((2, rounds, (tall + 2 * HALO) // 8, 8, LANES)),
            f32((count, 2, rounds, (width + 4 * HALO) // 8 + 1, 8, LANES)),
            f32(strip), f32(strip), f32(side), f32(side), f32(corner),
            f32(strip), f32(strip), f32(side), f32(side), f32(corner), f32(corner),
            dma((4 + count,)), dma((layers,)),
            dma((2, layers, 2, 2)), dma((2, layers, 2)), dma((2, layers, 2)),
            dma((2, layers, 2, 2)), dma((2, layers, 2)), dma((2, layers, 2)),
        ],
        compiler_params=pltpu.CompilerParams(collective_id=0, has_side_effects=True, vmem_limit_bytes=54 * 2**20),
    )(positions, object_slices, intensities.reshape(count, width, width), probe, propagator, tables)
    like = jax.ShapeDtypeStruct(object_slices.shape, object_slices.dtype)
    return tuple(
        pl.pallas_call(
            publish_kernel,
            out_shape=[like, like],
            in_specs=[pl.BlockSpec(memory_space=pltpu.VMEM)] * 2,
            out_specs=[anywhere] * 2,
            scratch_shapes=[dma((2,))],
            compiler_params=pltpu.CompilerParams(vmem_limit_bytes=2**20),
        )(*(pltpu.with_memory_space_constraint(v, pltpu.VMEM) for v in found))
    )


def solution(mesh):
    return jax.shard_map(
        on_device,
        mesh=mesh,
        in_specs=(
            P(None, None, "row", "col"),
            P("row", "col", None, None),
            P("row", "col", None, None, None),
            P(),
            P(),
        ),
        out_specs=(P(None, None, "row", "col"), P(None, None, "row", "col")),
        check_vma=False,
    )
```

```python
import functools

import jax
import jax.numpy as jnp
import numpy as np
from jax import lax
from jax.experimental import pallas as pl
from jax.experimental.pallas import tpu as pltpu
from jax.sharding import PartitionSpec as P

HALO = 64
LANES = 128

descent_rate = 0.5


def split(value):
    high = value.astype(jnp.bfloat16)
    low = (value - high.astype(jnp.float32)).astype(jnp.bfloat16)
    return high, low


def half_tables(width):
    half = width // 2
    place = np.arange(half)
    found = []
    for odd in (0, 1):
        angle = 2.0 * np.pi * (np.outer(2 * place + odd, place) % width) / width
        re = np.cos(angle) / np.sqrt(width)
        im = -np.sin(angle) / np.sqrt(width)
        found.append(np.block([[re, -im], [im, re]]).astype(np.float32))
    even, odd = found
    order = np.eye(width, dtype=np.float32)[np.concatenate([2 * place, 2 * place + 1])]
    six = np.stack([even, odd, even.T, odd.T, order, order.T])
    high = six.astype(jnp.bfloat16)
    low = (six - high.astype(np.float32)).astype(jnp.bfloat16)
    return np.stack([high, low])


def dot_left(pair, value):
    high, low = split(value)
    matrix = jnp.concatenate([pair[0], pair[0], pair[1]], 1)
    return jnp.dot(matrix, jnp.concatenate([high, low, high], 0), preferred_element_type=jnp.float32)


def dot_right(value, pair):
    high, low = split(value)
    matrix = jnp.concatenate([pair[0], pair[0], pair[1]], 0)
    return jnp.dot(jnp.concatenate([high, low, high], 1), matrix, preferred_element_type=jnp.float32)


def cut(value, dim):
    half = value.shape[dim] // 2
    return (lax.slice_in_dim(value, 0, half, axis=dim), lax.slice_in_dim(value, half, 2 * half, axis=dim))


def joined(first, second, dim):
    return jnp.concatenate([first, second], dim)


def forward_axis(re, im, dim, dot, even_matrix, odd_matrix):
    r0, r1 = cut(re, dim)
    i0, i1 = cut(im, dim)
    even_re, even_im = cut(dot(joined(r0 + r1, i0 + i1, dim), even_matrix), dim)
    odd_re, odd_im = cut(dot(joined(r0 - r1, i0 - i1, dim), odd_matrix), dim)
    return joined(even_re, odd_re, dim), joined(even_im, odd_im, dim)


def inverse_axis(re, im, dim, dot, even_matrix, odd_matrix):
    r0, r1 = cut(re, dim)
    i0, i1 = cut(im, dim)
    p_re, p_im = cut(dot(joined(r0, i0, dim), even_matrix), dim)
    q_re, q_im = cut(dot(joined(r1, i1, dim), odd_matrix), dim)
    return joined(p_re + q_re, p_re - q_re, dim), joined(p_im + q_im, p_im - q_im, dim)


def left_dot(value, pair):
    return dot_left(pair, value)


def turned_over(value, width, source, target):
    parts = [lax.slice_in_dim(value, at, at + width, axis=source) for at in range(0, value.shape[source], width)]
    return jnp.concatenate(parts, target)


def forward(re, im, pairs):
    width = re.shape[0]
    re, im = forward_axis(re, im, 0, left_dot, pairs(0), pairs(1))
    re, im = (turned_over(v, width, 1, 0) for v in (re, im))
    return forward_axis(re, im, 1, dot_right, pairs(2), pairs(3))


def inverse(re, im, pairs):
    width = re.shape[1]
    re, im = inverse_axis(re, im, 1, dot_right, pairs(0), pairs(1))
    re, im = (turned_over(v, width, 0, 1) for v in (re, im))
    return inverse_axis(re, im, 0, left_dot, pairs(2), pairs(3))


def hop(fields, phase_re, phase_im, pairs):
    width = fields[0][0].shape[0]
    re, im = forward(*(jnp.concatenate([f[c] for f in fields], 1) for c in range(2)), pairs)
    re, im = complex_product(re, im, *(jnp.concatenate([p] * len(fields), 0) for p in (phase_re, phase_im)))
    re, im = inverse(re, im, pairs)
    spans = [slice(at, at + width) for at in range(0, re.shape[1], width)]
    return [(re[:, span], im[:, span]) for span in spans]


def by_parity(value, left, right):
    rows = jnp.dot(
        jnp.concatenate([left, left], 1), jnp.concatenate(split(value), 0), preferred_element_type=jnp.float32
    )
    return jnp.dot(
        jnp.concatenate(split(rows), 1), jnp.concatenate([right, right], 0), preferred_element_type=jnp.float32
    )


def complex_product(left_re, left_im, right_re, right_im):
    return (left_re * right_re - left_im * right_im, left_re * right_im + left_im * right_re)


def slid(whole, shift, axis, span):
    turned = pltpu.roll(whole, lax.rem(span - shift, span), axis)
    kept = lax.broadcasted_iota(jnp.int32, whole[:-1].shape, axis) < span - shift
    return jnp.where(kept, turned[:-1], turned[1:])


def spread(whole, shift, axis, span):
    turned = pltpu.roll(whole, lax.rem(shift, span), axis)
    zero = jnp.zeros_like(turned[:1])
    first = jnp.concatenate([zero, turned], 0)
    other = jnp.concatenate([turned, zero], 0)
    moved = lax.broadcasted_iota(jnp.int32, first.shape, axis) < shift
    return jnp.where(moved, first, other)


def row_place(oy, rows, width):
    base = jnp.minimum(lax.div(oy, 8), (rows - width) // 8 - 1)
    return base, oy - 8 * base


def lane_place(ox):
    early = ox < HALO
    return jnp.where(early, 2, 0), jnp.where(early, ox + LANES - HALO, ox - HALO)


def swapped(value):
    return pltpu.roll(value, HALO, value.ndim - 1)


def choose(low, high):
    lower = lax.broadcasted_iota(jnp.int32, low.shape, low.ndim - 1) < HALO
    return jnp.where(lower, low, high)


def ends_of(cells):
    (re0, re1), (im0, im1) = cells
    return choose(re0, swapped(im0)), choose(swapped(re1), im1)


def middle_of(cells):
    return [choose(swapped(first), swapped(second)) for first, second in cells]


def unpacked(head, tail, middle_re, middle_im):
    mid_re, mid_im = swapped(middle_re), swapped(middle_im)
    return (
        (choose(head, mid_re), choose(mid_re, swapped(tail))),
        (choose(swapped(head), mid_im), choose(mid_im, tail)),
    )


def step_kernel(
    offsets_in, objects, intensities, probe, propagator, tables_in,
    gradient, updated,
    offsets, tables, cells, measured, ordered, phase, phases, waves, windows, slab, spans,
    row_out, row_in, col_out, col_in, corner_in,
    grow_out, grow_in, gcol_out, gcol_in, gcorner_out, gcorner_in,
    load_sem, slice_sem, row_sem, col_sem, corner_sem, grow_sem, gcol_sem, gcorner_sem,
):
    count, width = measured.shape[0], measured.shape[-1]
    layers, tall = cells.shape[1:3]
    last = layers - 1
    wide = cells.shape[3] // LANES
    rounds = wide + 1
    whole = tall + 2 * HALO
    pad = 2 * HALO

    rows_n, cols_n = lax.axis_size("row"), lax.axis_size("col")
    row, col = lax.axis_index("row"), lax.axis_index("col")
    below, above = lax.rem(row + 1, rows_n), lax.rem(row + rows_n - 1, rows_n)
    right, left = lax.rem(col + 1, cols_n), lax.rem(col + cols_n - 1, cols_n)
    row_to = ((below, col), (above, col))
    col_to = ((row, right), (row, left))

    def send(src, dst, sems, where, target):
        return pltpu.make_async_remote_copy(
            src_ref=src, dst_ref=dst, send_sem=sems.at[(0, *where)], recv_sem=sems.at[(1, *where)],
            device_id=target, device_id_type=pl.DeviceIdType.MESH,
        )

    def row_copy(layer, half, d):
        where = (layer, half, slice(None), d)
        target = (lax.rem(row + rows_n + 1 - 2 * d, rows_n), col)
        return send(row_out.at[where], row_in.at[where], row_sem, (layer, half, d), target)

    def col_copy(layer, side):
        return send(col_out.at[layer, side], col_in.at[layer, side], col_sem, (layer, side), col_to[side])

    def corner_copy(layer, side):
        source = row_in.at[layer, 0, 1 - side]
        return send(source, corner_in.at[layer, side], corner_sem, (layer, side), col_to[side])

    def grow_copy(layer, half, d):
        where = (layer, half, slice(None), d)
        target = (lax.rem(row + rows_n + 1 - 2 * d, rows_n), col)
        return send(grow_out.at[where], grow_in.at[where], grow_sem, (layer, half, d), target)

    def gcol_copy(layer, side):
        return send(gcol_out.at[layer, side], gcol_in.at[layer, side], gcol_sem, (layer, side), col_to[side])

    def gcorner_copy(layer, side):
        return send(
            gcorner_out.at[layer, side], gcorner_in.at[layer, side], gcorner_sem, (layer, side), col_to[side]
        )

    loads = [
        pltpu.make_async_copy(propagator, phase, load_sem.at[0]),
        pltpu.make_async_copy(tables_in, tables, load_sem.at[1]),
        pltpu.make_async_copy(intensities, measured, load_sem.at[2]),
        pltpu.make_async_copy(offsets_in, offsets, load_sem.at[3]),
    ] + [pltpu.make_async_copy(probe, waves.at[k, 0], load_sem.at[4 + k]) for k in range(count)]

    def slice_load(layer):
        return pltpu.make_async_copy(objects.at[:, layer], cells.at[:, layer], slice_sem.at[layer])

    barrier = pltpu.get_barrier_semaphore()
    for target in row_to + col_to:
        pl.semaphore_signal(barrier, inc=1, device_id=target, device_id_type=pl.DeviceIdType.MESH)
    for layer in range(layers):
        slice_load(layer).start()

    def lane_blocks(ref, layer, rows):
        return [[ref[c, layer, rows, pl.ds(j * LANES, LANES)] for j in range(wide)] for c in range(2)]

    def pack(layer):
        slice_load(layer).wait()
        for d, at in enumerate((tall - HALO, 0)):
            strip = lane_blocks(cells, layer, pl.ds(at, HALO))
            for half, packs in enumerate((ends_of(strip), middle_of(strip))):
                for i in range(2):
                    row_out[layer, half, i, d] = packs[i]
        head, tail = ends_of(lane_blocks(cells, layer, pl.ds(0, tall)))
        col_out[layer, 0] = tail
        col_out[layer, 1] = head

    def launch(layer):
        for half in range(2):
            for d in range(2):
                row_copy(layer, half, d).start()

    def pack_and_launch(layer, carry):
        pack(layer)
        launch(layer)
        launch_sides(layer)
        return carry

    def launch_sides(layer):
        for side in range(2):
            col_copy(layer, side).start()

    pack(0)
    pl.semaphore_wait(barrier, 4)
    launch(0)
    launch_sides(0)
    for load in loads:
        load.start()
    lax.fori_loop(1, layers, pack_and_launch, 0)

    def pairs(index):
        return tables[0, index], tables[1, index]

    for load in loads:
        load.wait()
    angle = phase[...]
    phases[0] = by_parity(jnp.cos(angle), tables[0, 4], tables[0, 5])
    phases[1] = by_parity(jnp.sin(angle), tables[0, 4], tables[0, 5])
    for k in range(count):
        ordered[k] = by_parity(measured[k], tables[0, 4], tables[0, 5])
    blank = jnp.zeros((pad // 8, 8, LANES), jnp.float32)
    for k in range(count):
        for c in range(2):
            for j in range(rounds):
                spans[k, c, j, pl.ds(0, pad // 8)] = blank
                spans[k, c, j, pl.ds((pad + width) // 8 + 1, pad // 8)] = blank

    def forward_corners(layer, more):
        for d in range(2):
            row_copy(layer, 0, d).wait_recv()
        for side in range(2):
            corner_copy(layer, side).start()
        if more:
            launch_sides(layer + 1)

    def assemble(layer):
        def place(start, size, blocks, l, r):
            rows, tiles = pl.ds(start // 8, size // 8), (size // 8, 8, LANES)
            for c in range(2):
                for j in range(wide):
                    slab[c, j, rows] = blocks[c][j].reshape(tiles)
            slab[0, wide, rows] = choose(r, swapped(l)).reshape(tiles)
            slab[1, wide, rows] = choose(swapped(r), l).reshape(tiles)

        for side in range(2):
            col_copy(layer, side).wait_recv()
        place(HALO, tall, lane_blocks(cells, layer, pl.ds(0, tall)), col_in[layer, 0], col_in[layer, 1])
        for d in range(2):
            row_copy(layer, 1, d).wait_recv()
        for side in range(2):
            corner_copy(layer, side).wait_recv()
        for d, start in enumerate((0, HALO + tall)):
            blocks = unpacked(*(row_in[layer, half, i, d] for half in range(2) for i in range(2)))
            place(start, HALO, blocks, corner_in[layer, 0, d], corner_in[layer, 1, d])

    def cut_layer(k, layer):
        base, shift = row_place(offsets[0, 0, k, 0], whole, width)
        first, turn = lane_place(offsets[0, 0, k, 1])
        for c in range(2):
            blocks = jnp.stack(
                [slab[c, lax.rem(first + j, rounds), pl.ds(base, width // 8 + 1)] for j in range(rounds)]
            )
            blocks = slid(blocks, turn, 3, LANES)
            for j in range(wide):
                part = slid(blocks[j], shift, 1, 8)
                windows[k, layer, c, :, j * LANES : j * LANES + LANES] = part.reshape(width, LANES)

    def leave(k, layer):
        return complex_product(
            waves[k, layer, 0], waves[k, layer, 1], windows[k, layer, 0], windows[k, layer, 1]
        )

    def onward(layer, carry):
        assemble(layer)
        for k in range(count):
            cut_layer(k, layer)
            if k == 0:
                forward_corners(layer + 1, False)
            ((re, im),) = hop([leave(k, layer)], phases[0], phases[1], pairs)
            waves[k, layer + 1, 0] = re
            waves[k, layer + 1, 1] = im
        return carry

    forward_corners(0, False)
    lax.fori_loop(0, last, onward, 0)

    def record(k, layer, back_re, back_im):
        wave_re, wave_im = waves[k, layer, 0], waves[k, layer, 1]
        shift = row_place(offsets[0, 0, k, 0], whole, width)[1]
        turn = lane_place(offsets[0, 0, k, 1])[1]
        terms = (wave_re * back_re + wave_im * back_im, wave_re * back_im - wave_im * back_re)
        for c in range(2):
            blocks = jnp.stack([terms[c][:, j * LANES : j * LANES + LANES] for j in range(wide)])
            blocks = spread(blocks, turn, 2, LANES)
            for j in range(rounds):
                part = spread(blocks[j].reshape(width // 8, 8, LANES), shift, 1, 8)
                spans[k, c, j, pl.ds(pad // 8, width // 8 + 1)] = part

    def summed(c, block, start, size):
        found = None
        for k in range(count):
            base = row_place(offsets[0, 0, k, 0], whole, width)[0]
            first = lane_place(offsets[0, 0, k, 1])[0]
            at = (pad + start) // 8 - base
            term = spans[k, c, lax.rem(block + rounds - first, rounds), pl.ds(at, size // 8)]
            found = term if found is None else found + term
        return found.reshape(size, LANES)

    def settle(layer):
        def sums(start, size):
            blocks = [[summed(c, j, start, size) for j in range(wide)] for c in range(2)]
            outer_re, outer_im = (summed(c, wide, start, size) for c in range(2))
            return blocks, (choose(outer_re, swapped(outer_im)), choose(swapped(outer_re), outer_im))

        for d, start in enumerate((0, HALO + tall)):
            blocks, outer = sums(start, HALO)
            for half, packs in enumerate((ends_of(blocks), middle_of(blocks))):
                for i in range(2):
                    grow_out[layer, half, i, 1 - d] = packs[i]
            for side in range(2):
                gcorner_out[layer, side, 1 - d] = outer[side]
        for side in range(2):
            gcorner_copy(layer, side).start()
        for d in range(2):
            grow_copy(layer, 1, d).start()

        blocks, outer = sums(HALO, tall)
        for c in range(2):
            for j in range(wide):
                gradient[c, layer, :, j * LANES : j * LANES + LANES] = blocks[c][j]
        for side in range(2):
            gcol_out[layer, side] = outer[side]
            gcol_copy(layer, side).start()

    def pass_on(layer):
        for side in range(2):
            gcorner_copy(layer, side).wait_recv()
        for d in range(2):
            for side in range(2):
                grow_out[layer, 0, side, d] += gcorner_in[layer, side, d]
        for d in range(2):
            grow_copy(layer, 0, d).start()

    assemble(last)
    for k in range(count):
        cut_layer(k, last)
    leaving = [leave(k, last) for k in range(count)]
    far_re, far_im = forward(*(jnp.concatenate([v[c] for v in leaving], 1) for c in range(2)), pairs)
    misfit = far_re * far_re + far_im * far_im - ordered[...].reshape(far_re.shape)
    backs = inverse(misfit * far_re, misfit * far_im, pairs)
    for k in range(count):
        back_re, back_im = (v[:, k * width : (k + 1) * width] for v in backs)
        record(k, last, back_re, back_im)
        waves[k, last, 0] = back_re
        waves[k, last, 1] = back_im
    settle(last)

    def backward(step, carry):
        layer = last - step
        fields = []
        for k in range(count):
            back_re, back_im = waves[k, layer, 0], waves[k, layer, 1]
            slab_re, slab_im = windows[k, layer, 0], windows[k, layer, 1]
            fields.append(complex_product(back_re, back_im, slab_re, -slab_im))
        backs = hop(fields, phases[0], -phases[1], pairs)
        pass_on(layer)
        for k, (re, im) in enumerate(backs):
            record(k, layer - 1, re, im)
            waves[k, layer - 1, 0] = re
            waves[k, layer - 1, 1] = im
        settle(layer - 1)
        return carry

    lax.fori_loop(0, last, backward, 0)
    pass_on(0)
    def finish(step, carry):
        layer = last - step
        for side in range(2):
            gcol_copy(layer, side).wait_recv()
        for half in (1, 0):
            for d in range(2):
                grow_copy(layer, half, d).wait_recv()
        spots = ((0, HALO, 0), (HALO, tall - 2 * HALO, None), (tall - HALO, HALO, 1))
        for start, size, d in spots:
            rows = pl.ds(start, size)
            sums = lane_blocks(gradient, layer, rows)
            if d is not None:
                added = unpacked(*(grow_in[layer, half, i, d] for half in range(2) for i in range(2)))
                sums = [[sums[c][j] + added[c][j] for j in range(wide)] for c in range(2)]
            l, r = gcol_in[layer, 0, rows, :], gcol_in[layer, 1, rows, :]
            zero = jnp.zeros_like(l)
            sums[0][0] += choose(l, zero)
            sums[1][0] += choose(swapped(l), zero)
            sums[0][wide - 1] += choose(zero, swapped(r))
            sums[1][wide - 1] += choose(zero, r)
            for c in range(2):
                for j in range(wide):
                    lanes = pl.ds(j * LANES, LANES)
                    gradient[c, layer, rows, lanes] = sums[c][j]
                    updated[c, layer, rows, lanes] = cells[c, layer, rows, lanes] - descent_rate * sums[c][j]
        return carry

    lax.fori_loop(0, layers, finish, 0)

    def close(layer, carry):
        for d in range(2):
            for half in range(2):
                row_copy(layer, half, d).wait_send()
                grow_copy(layer, half, d).wait_send()
            col_copy(layer, d).wait_send()
            corner_copy(layer, d).wait_send()
            gcol_copy(layer, d).wait_send()
            gcorner_copy(layer, d).wait_send()
        return carry

    lax.fori_loop(0, layers, close, 0)


def publish_kernel(gradient, updated, gradient_out, updated_out, sems):
    copies = [
        pltpu.make_async_copy(held.at[:, layer], out.at[:, layer], sems.at[i, layer])
        for i, (held, out) in enumerate(((gradient, gradient_out), (updated, updated_out)))
        for layer in range(gradient.shape[1])
    ]
    for copy in copies:
        copy.start()
    for copy in copies:
        copy.wait()


def on_device(object_slices, positions, intensities, probe, propagator):
    count, width = intensities.shape[2], intensities.shape[-1]
    layers, tall, broad = object_slices.shape[1:]
    rounds = broad // LANES + 1
    tables = jnp.asarray(half_tables(width))
    anywhere = pl.BlockSpec(memory_space=pl.ANY)
    f32 = functools.partial(pltpu.VMEM, dtype=jnp.float32)
    strip, side, corner = (layers, 2, 2, 2, HALO, LANES), (layers, 2, tall, LANES), (layers, 2, 2, HALO, LANES)
    dma = pltpu.SemaphoreType.DMA
    held = pltpu.VMEM(object_slices.shape, object_slices.dtype)
    pair = [held, held]
    found = pl.pallas_call(
        step_kernel,
        out_shape=pair,
        in_specs=[anywhere] * 6,
        out_specs=[pl.BlockSpec(memory_space=pltpu.VMEM)] * 2,
        scratch_shapes=[
            pltpu.SMEM(positions.shape, positions.dtype),
            pltpu.VMEM(tables.shape, tables.dtype),
            f32(object_slices.shape),
            f32((count, width, width)),
            f32((count, width, width)),
            f32((width, width)),
            f32((2, width, width)),
            f32((count, layers, 2, width, width)),
            f32((count, layers, 2, width, width)),
            f32((2, rounds, (tall + 2 * HALO) // 8, 8, LANES)),
            f32((count, 2, rounds, (width + 4 * HALO) // 8 + 1, 8, LANES)),
            f32(strip), f32(strip), f32(side), f32(side), f32(corner),
            f32(strip), f32(strip), f32(side), f32(side), f32(corner), f32(corner),
            dma((4 + count,)), dma((layers,)),
            dma((2, layers, 2, 2)), dma((2, layers, 2)), dma((2, layers, 2)),
            dma((2, layers, 2, 2)), dma((2, layers, 2)), dma((2, layers, 2)),
        ],
        compiler_params=pltpu.CompilerParams(collective_id=0, has_side_effects=True, vmem_limit_bytes=54 * 2**20),
    )(positions, object_slices, intensities.reshape(count, width, width), probe, propagator, tables)
    like = jax.ShapeDtypeStruct(object_slices.shape, object_slices.dtype)
    return tuple(
        pl.pallas_call(
            publish_kernel,
            out_shape=[like, like],
            in_specs=[pl.BlockSpec(memory_space=pltpu.VMEM)] * 2,
            out_specs=[anywhere] * 2,
            scratch_shapes=[dma((2, layers))],
            compiler_params=pltpu.CompilerParams(vmem_limit_bytes=2**20),
        )(*(pltpu.with_memory_space_constraint(v, pltpu.VMEM) for v in found))
    )


def solution(mesh):
    return jax.shard_map(
        on_device,
        mesh=mesh,
        in_specs=(
            P(None, None, "row", "col"),
            P("row", "col", None, None),
            P("row", "col", None, None, None),
            P(),
            P(),
        ),
        out_specs=(P(None, None, "row", "col"), P(None, None, "row", "col")),
        check_vma=False,
    )
```

```python
import functools

import jax
import jax.numpy as jnp
import numpy as np
from jax import lax
from jax.experimental import pallas as pl
from jax.experimental.pallas import tpu as pltpu
from jax.sharding import PartitionSpec as P

HALO = 64
LANES = 128

descent_rate = 0.5


def split(value):
    high = value.astype(jnp.bfloat16)
    low = (value - high.astype(jnp.float32)).astype(jnp.bfloat16)
    return high, low


def half_tables(width):
    half = width // 2
    place = np.arange(half)
    found = []
    for odd in (0, 1):
        angle = 2.0 * np.pi * (np.outer(2 * place + odd, place) % width) / width
        re = np.cos(angle) / np.sqrt(width)
        im = -np.sin(angle) / np.sqrt(width)
        found.append(np.block([[re, -im], [im, re]]).astype(np.float32))
    even, odd = found
    order = np.eye(width, dtype=np.float32)[np.concatenate([2 * place, 2 * place + 1])]
    six = np.stack([even, odd, even.T, odd.T, order, order.T])
    high = six.astype(jnp.bfloat16)
    low = (six - high.astype(np.float32)).astype(jnp.bfloat16)
    return np.stack([high, low])


def dot_left(pair, value):
    high, low = split(value)
    matrix = jnp.concatenate([pair[0], pair[0], pair[1]], 1)
    return jnp.dot(matrix, jnp.concatenate([high, low, high], 0), preferred_element_type=jnp.float32)


def dot_right(value, pair):
    high, low = split(value)
    matrix = jnp.concatenate([pair[0], pair[0], pair[1]], 0)
    return jnp.dot(jnp.concatenate([high, low, high], 1), matrix, preferred_element_type=jnp.float32)


def cut(value, dim):
    half = value.shape[dim] // 2
    return (lax.slice_in_dim(value, 0, half, axis=dim), lax.slice_in_dim(value, half, 2 * half, axis=dim))


def joined(first, second, dim):
    return jnp.concatenate([first, second], dim)


def forward_axis(re, im, dim, dot, even_matrix, odd_matrix):
    r0, r1 = cut(re, dim)
    i0, i1 = cut(im, dim)
    even_re, even_im = cut(dot(joined(r0 + r1, i0 + i1, dim), even_matrix), dim)
    odd_re, odd_im = cut(dot(joined(r0 - r1, i0 - i1, dim), odd_matrix), dim)
    return joined(even_re, odd_re, dim), joined(even_im, odd_im, dim)


def inverse_axis(re, im, dim, dot, even_matrix, odd_matrix):
    r0, r1 = cut(re, dim)
    i0, i1 = cut(im, dim)
    p_re, p_im = cut(dot(joined(r0, i0, dim), even_matrix), dim)
    q_re, q_im = cut(dot(joined(r1, i1, dim), odd_matrix), dim)
    return joined(p_re + q_re, p_re - q_re, dim), joined(p_im + q_im, p_im - q_im, dim)


def left_dot(value, pair):
    return dot_left(pair, value)


def turned_over(value, width, source, target):
    parts = [lax.slice_in_dim(value, at, at + width, axis=source) for at in range(0, value.shape[source], width)]
    return jnp.concatenate(parts, target)


def forward(re, im, pairs):
    width = re.shape[0]
    re, im = forward_axis(re, im, 0, left_dot, pairs(0), pairs(1))
    re, im = (turned_over(v, width, 1, 0) for v in (re, im))
    return forward_axis(re, im, 1, dot_right, pairs(2), pairs(3))


def inverse(re, im, pairs):
    width = re.shape[1]
    re, im = inverse_axis(re, im, 1, dot_right, pairs(0), pairs(1))
    re, im = (turned_over(v, width, 0, 1) for v in (re, im))
    return inverse_axis(re, im, 0, left_dot, pairs(2), pairs(3))


def hop(fields, phase_re, phase_im, pairs):
    width = fields[0][0].shape[0]
    re, im = forward(*(jnp.concatenate([f[c] for f in fields], 1) for c in range(2)), pairs)
    re, im = complex_product(re, im, *(jnp.concatenate([p] * len(fields), 0) for p in (phase_re, phase_im)))
    re, im = inverse(re, im, pairs)
    spans = [slice(at, at + width) for at in range(0, re.shape[1], width)]
    return [(re[:, span], im[:, span]) for span in spans]


def by_parity(value, left, right):
    rows = jnp.dot(
        jnp.concatenate([left, left], 1), jnp.concatenate(split(value), 0), preferred_element_type=jnp.float32
    )
    return jnp.dot(
        jnp.concatenate(split(rows), 1), jnp.concatenate([right, right], 0), preferred_element_type=jnp.float32
    )


def complex_product(left_re, left_im, right_re, right_im):
    return (left_re * right_re - left_im * right_im, left_re * right_im + left_im * right_re)


def slid(whole, shift, axis, span):
    turned = pltpu.roll(whole, lax.rem(span - shift, span), axis)
    kept = lax.broadcasted_iota(jnp.int32, whole[:-1].shape, axis) < span - shift
    return jnp.where(kept, turned[:-1], turned[1:])


def spread(whole, shift, axis, span):
    turned = pltpu.roll(whole, lax.rem(shift, span), axis)
    zero = jnp.zeros_like(turned[:1])
    first = jnp.concatenate([zero, turned], 0)
    other = jnp.concatenate([turned, zero], 0)
    moved = lax.broadcasted_iota(jnp.int32, first.shape, axis) < shift
    return jnp.where(moved, first, other)


def row_place(oy, rows, width):
    base = jnp.minimum(lax.div(oy, 8), (rows - width) // 8 - 1)
    return base, oy - 8 * base


def lane_place(ox):
    early = ox < HALO
    return jnp.where(early, 2, 0), jnp.where(early, ox + LANES - HALO, ox - HALO)


def swapped(value):
    return pltpu.roll(value, HALO, value.ndim - 1)


def choose(low, high):
    lower = lax.broadcasted_iota(jnp.int32, low.shape, low.ndim - 1) < HALO
    return jnp.where(lower, low, high)


def ends_of(cells):
    (re0, re1), (im0, im1) = cells
    return choose(re0, swapped(im0)), choose(swapped(re1), im1)


def middle_of(cells):
    return [choose(swapped(first), swapped(second)) for first, second in cells]


def unpacked(head, tail, middle_re, middle_im):
    mid_re, mid_im = swapped(middle_re), swapped(middle_im)
    return (
        (choose(head, mid_re), choose(mid_re, swapped(tail))),
        (choose(swapped(head), mid_im), choose(mid_im, tail)),
    )


def step_kernel(
    offsets_in, objects, intensities, probe, propagator, tables_in,
    gradient, updated,
    offsets, tables, cells, measured, ordered, phase, phases, waves, windows, slab, spans,
    row_out, row_in, col_out, col_in, corner_in,
    grow_out, grow_in, gcol_out, gcol_in, gcorner_out, gcorner_in,
    load_sem, slice_sem, row_sem, col_sem, corner_sem, grow_sem, gcol_sem, gcorner_sem,
):
    count, width = measured.shape[0], measured.shape[-1]
    layers, tall = cells.shape[1:3]
    last = layers - 1
    wide = cells.shape[3] // LANES
    rounds = wide + 1
    whole = tall + 2 * HALO
    pad = 2 * HALO

    rows_n, cols_n = lax.axis_size("row"), lax.axis_size("col")
    row, col = lax.axis_index("row"), lax.axis_index("col")
    below, above = lax.rem(row + 1, rows_n), lax.rem(row + rows_n - 1, rows_n)
    right, left = lax.rem(col + 1, cols_n), lax.rem(col + cols_n - 1, cols_n)
    row_to = ((below, col), (above, col))
    col_to = ((row, right), (row, left))

    def send(src, dst, sems, where, target):
        return pltpu.make_async_remote_copy(
            src_ref=src, dst_ref=dst, send_sem=sems.at[(0, *where)], recv_sem=sems.at[(1, *where)],
            device_id=target, device_id_type=pl.DeviceIdType.MESH,
        )

    def row_copy(layer, half, d):
        where = (layer, half, slice(None), d)
        target = (lax.rem(row + rows_n + 1 - 2 * d, rows_n), col)
        return send(row_out.at[where], row_in.at[where], row_sem, (layer, half, d), target)

    def col_copy(layer, side):
        return send(col_out.at[layer, side], col_in.at[layer, side], col_sem, (layer, side), col_to[side])

    def corner_copy(layer, side):
        source = row_in.at[layer, 0, 1 - side]
        return send(source, corner_in.at[layer, side], corner_sem, (layer, side), col_to[side])

    def grow_copy(layer, half, d):
        where = (layer, half, slice(None), d)
        target = (lax.rem(row + rows_n + 1 - 2 * d, rows_n), col)
        return send(grow_out.at[where], grow_in.at[where], grow_sem, (layer, half, d), target)

    def gcol_copy(layer, side):
        return send(gcol_out.at[layer, side], gcol_in.at[layer, side], gcol_sem, (layer, side), col_to[side])

    def gcorner_copy(layer, side):
        return send(
            gcorner_out.at[layer, side], gcorner_in.at[layer, side], gcorner_sem, (layer, side), col_to[side]
        )

    loads = [
        pltpu.make_async_copy(propagator, phase, load_sem.at[0]),
        pltpu.make_async_copy(tables_in, tables, load_sem.at[1]),
        pltpu.make_async_copy(intensities, measured, load_sem.at[2]),
        pltpu.make_async_copy(offsets_in, offsets, load_sem.at[3]),
    ] + [pltpu.make_async_copy(probe, waves.at[k, 0], load_sem.at[4 + k]) for k in range(count)]

    def slice_load(layer):
        return pltpu.make_async_copy(objects.at[:, layer], cells.at[:, layer], slice_sem.at[layer])

    barrier = pltpu.get_barrier_semaphore()
    for target in row_to + col_to:
        pl.semaphore_signal(barrier, inc=1, device_id=target, device_id_type=pl.DeviceIdType.MESH)
    for layer in range(layers):
        slice_load(layer).start()

    def lane_blocks(ref, layer, rows):
        return [[ref[c, layer, rows, pl.ds(j * LANES, LANES)] for j in range(wide)] for c in range(2)]

    def pack(layer):
        slice_load(layer).wait()
        for d, at in enumerate((tall - HALO, 0)):
            strip = lane_blocks(cells, layer, pl.ds(at, HALO))
            for half, packs in enumerate((ends_of(strip), middle_of(strip))):
                for i in range(2):
                    row_out[layer, half, i, d] = packs[i]
        head, tail = ends_of(lane_blocks(cells, layer, pl.ds(0, tall)))
        col_out[layer, 0] = tail
        col_out[layer, 1] = head

    def launch(layer):
        for d in range(2):
            for half in range(2):
                row_copy(layer, half, d).start()

    def pack_and_launch(layer, carry):
        pack(layer)
        launch(layer)
        launch_sides(layer)
        return carry

    def launch_sides(layer):
        for side in range(2):
            col_copy(layer, side).start()

    pack(0)
    pl.semaphore_wait(barrier, 4)
    launch(0)
    launch_sides(0)
    for load in loads:
        load.start()
    lax.fori_loop(1, layers, pack_and_launch, 0)

    def pairs(index):
        return tables[0, index], tables[1, index]

    for load in loads:
        load.wait()
    angle = phase[...]
    phases[0] = by_parity(jnp.cos(angle), tables[0, 4], tables[0, 5])
    phases[1] = by_parity(jnp.sin(angle), tables[0, 4], tables[0, 5])
    for k in range(count):
        ordered[k] = by_parity(measured[k], tables[0, 4], tables[0, 5])
    blank = jnp.zeros((pad // 8, 8, LANES), jnp.float32)
    for k in range(count):
        for c in range(2):
            for j in range(rounds):
                spans[k, c, j, pl.ds(0, pad // 8)] = blank
                spans[k, c, j, pl.ds((pad + width) // 8 + 1, pad // 8)] = blank

    def forward_corners(layer):
        for d in range(2):
            row_copy(layer, 0, d).wait_recv()
        for side in range(2):
            corner_copy(layer, side).start()

    def assemble(layer):
        def place(start, size, blocks, l, r):
            rows, tiles = pl.ds(start // 8, size // 8), (size // 8, 8, LANES)
            for c in range(2):
                for j in range(wide):
                    slab[c, j, rows] = blocks[c][j].reshape(tiles)
            slab[0, wide, rows] = choose(r, swapped(l)).reshape(tiles)
            slab[1, wide, rows] = choose(swapped(r), l).reshape(tiles)

        for side in range(2):
            col_copy(layer, side).wait_recv()
        place(HALO, tall, lane_blocks(cells, layer, pl.ds(0, tall)), col_in[layer, 0], col_in[layer, 1])
        for d in range(2):
            row_copy(layer, 1, d).wait_recv()
        for side in range(2):
            corner_copy(layer, side).wait_recv()
        for d, start in enumerate((0, HALO + tall)):
            blocks = unpacked(*(row_in[layer, half, i, d] for half in range(2) for i in range(2)))
            place(start, HALO, blocks, corner_in[layer, 0, d], corner_in[layer, 1, d])

    def cut_layer(k, layer):
        base, shift = row_place(offsets[0, 0, k, 0], whole, width)
        first, turn = lane_place(offsets[0, 0, k, 1])
        for c in range(2):
            blocks = jnp.stack(
                [slab[c, lax.rem(first + j, rounds), pl.ds(base, width // 8 + 1)] for j in range(rounds)]
            )
            blocks = slid(blocks, turn, 3, LANES)
            for j in range(wide):
                part = slid(blocks[j], shift, 1, 8)
                windows[k, layer, c, :, j * LANES : j * LANES + LANES] = part.reshape(width, LANES)

    def leave(k, layer):
        return complex_product(
            waves[k, layer, 0], waves[k, layer, 1], windows[k, layer, 0], windows[k, layer, 1]
        )

    def onward(layer, carry):
        assemble(layer)
        for k in range(count):
            cut_layer(k, layer)
            if k == 0:
                forward_corners(layer + 1)
            ((re, im),) = hop([leave(k, layer)], phases[0], phases[1], pairs)
            waves[k, layer + 1, 0] = re
            waves[k, layer + 1, 1] = im
        return carry

    forward_corners(0)
    lax.fori_loop(0, last, onward, 0)

    def record(k, layer, back_re, back_im, start, stop):
        low, high = max(start - 1, 0), min(stop, width // 8)
        rows, span = pl.ds(8 * low, 8 * (high - low)), slice(8 * low, 8 * high)
        wave_re, wave_im = waves[k, layer, 0, rows, :], waves[k, layer, 1, rows, :]
        back_re, back_im = back_re[span], back_im[span]
        shift = row_place(offsets[0, 0, k, 0], whole, width)[1]
        turn = lane_place(offsets[0, 0, k, 1])[1]
        terms = (wave_re * back_re + wave_im * back_im, wave_re * back_im - wave_im * back_re)
        for c in range(2):
            blocks = jnp.stack([terms[c][:, j * LANES : j * LANES + LANES] for j in range(wide)])
            blocks = spread(blocks, turn, 2, LANES)
            for j in range(rounds):
                turned = pltpu.roll(blocks[j].reshape(high - low, 8, LANES), lax.rem(shift, 8), 1)
                zero = jnp.zeros_like(turned[:1])
                before, after = turned[: stop - 1 - low], turned[start - low :]
                if start == 0:
                    before = jnp.concatenate([zero, before], 0)
                if stop > high:
                    after = jnp.concatenate([after, zero], 0)
                else:
                    after = after[: stop - start]
                moved = lax.broadcasted_iota(jnp.int32, before.shape, 1) < shift
                spans[k, c, j, pl.ds(pad // 8 + start, stop - start)] = jnp.where(moved, before, after)

    def summed(c, block, start, size):
        found = None
        for k in range(count):
            base = row_place(offsets[0, 0, k, 0], whole, width)[0]
            first = lane_place(offsets[0, 0, k, 1])[0]
            at = (pad + start) // 8 - base
            term = spans[k, c, lax.rem(block + rounds - first, rounds), pl.ds(at, size // 8)]
            found = term if found is None else found + term
        return found.reshape(size, LANES)

    def sums(start, size):
        blocks = [[summed(c, j, start, size) for j in range(wide)] for c in range(2)]
        outer_re, outer_im = (summed(c, wide, start, size) for c in range(2))
        return blocks, (choose(outer_re, swapped(outer_im)), choose(swapped(outer_re), outer_im))

    def settle(layer, backs):
        reach = HALO // 8
        for k in range(count):
            record(k, layer, *backs[k], 0, reach)
            record(k, layer, *backs[k], width // 8 + 1 - reach, width // 8 + 1)
        for d, start in enumerate((0, HALO + tall)):
            blocks, outer = sums(start, HALO)
            for half, packs in enumerate((ends_of(blocks), middle_of(blocks))):
                for i in range(2):
                    grow_out[layer, half, i, 1 - d] = packs[i]
            for side in range(2):
                gcorner_out[layer, side, 1 - d] = outer[side]
        for d in range(2):
            grow_copy(layer, 1, d).start()
        for side in range(2):
            gcorner_copy(layer, side).start()
        for k in range(count):
            record(k, layer, *backs[k], reach, width // 8 + 1 - reach)
        blocks, outer = sums(HALO, tall)
        for c in range(2):
            for j in range(wide):
                gradient[c, layer, :, j * LANES : j * LANES + LANES] = blocks[c][j]
        for side in range(2):
            gcol_out[layer, side] = outer[side]
            gcol_copy(layer, side).start()
        for k in range(count):
            for c in range(2):
                waves[k, layer, c] = backs[k][c]

    def pass_on(layer):
        for side in range(2):
            gcorner_copy(layer, side).wait_recv()
        for d in range(2):
            for side in range(2):
                grow_out[layer, 0, side, d] += gcorner_in[layer, side, d]
        for d in range(2):
            grow_copy(layer, 0, d).start()

    assemble(last)
    for k in range(count):
        cut_layer(k, last)
    leaving = [leave(k, last) for k in range(count)]
    far_re, far_im = forward(*(jnp.concatenate([v[c] for v in leaving], 1) for c in range(2)), pairs)
    misfit = far_re * far_re + far_im * far_im - ordered[...].reshape(far_re.shape)
    backs = inverse(misfit * far_re, misfit * far_im, pairs)
    settle(last, [[v[:, k * width : (k + 1) * width] for v in backs] for k in range(count)])

    def backward(step, carry):
        layer = last - step
        fields = []
        for k in range(count):
            back_re, back_im = waves[k, layer, 0], waves[k, layer, 1]
            slab_re, slab_im = windows[k, layer, 0], windows[k, layer, 1]
            fields.append(complex_product(back_re, back_im, slab_re, -slab_im))
        backs = hop(fields, phases[0], -phases[1], pairs)
        pass_on(layer)
        settle(layer - 1, backs)
        return carry

    lax.fori_loop(0, last, backward, 0)
    pass_on(0)
    def close_in(layer, carry):
        for d in range(2):
            for half in range(2):
                row_copy(layer, half, d).wait_send()
            col_copy(layer, d).wait_send()
            corner_copy(layer, d).wait_send()
        return carry

    lax.fori_loop(0, layers, close_in, 0)

    def finish(step, carry):
        layer = last - step
        for side in range(2):
            gcol_copy(layer, side).wait_recv()
        for half in (1, 0):
            for d in range(2):
                grow_copy(layer, half, d).wait_recv()
        spots = ((0, HALO, 0), (HALO, tall - 2 * HALO, None), (tall - HALO, HALO, 1))
        for start, size, d in spots:
            rows = pl.ds(start, size)
            sums = lane_blocks(gradient, layer, rows)
            if d is not None:
                added = unpacked(*(grow_in[layer, half, i, d] for half in range(2) for i in range(2)))
                sums = [[sums[c][j] + added[c][j] for j in range(wide)] for c in range(2)]
            l, r = gcol_in[layer, 0, rows, :], gcol_in[layer, 1, rows, :]
            zero = jnp.zeros_like(l)
            sums[0][0] += choose(l, zero)
            sums[1][0] += choose(swapped(l), zero)
            sums[0][wide - 1] += choose(zero, swapped(r))
            sums[1][wide - 1] += choose(zero, r)
            for c in range(2):
                for j in range(wide):
                    lanes = pl.ds(j * LANES, LANES)
                    gradient[c, layer, rows, lanes] = sums[c][j]
                    updated[c, layer, rows, lanes] = cells[c, layer, rows, lanes] - descent_rate * sums[c][j]
        return carry

    lax.fori_loop(0, layers, finish, 0)

    def close_out(layer, carry):
        for d in range(2):
            for half in range(2):
                grow_copy(layer, half, d).wait_send()
            gcol_copy(layer, d).wait_send()
            gcorner_copy(layer, d).wait_send()
        return carry

    lax.fori_loop(0, layers, close_out, 0)


def publish_kernel(gradient, updated, gradient_out, updated_out, sems):
    copies = [
        pltpu.make_async_copy(held.at[:, layer], out.at[:, layer], sems.at[i, layer])
        for i, (held, out) in enumerate(((gradient, gradient_out), (updated, updated_out)))
        for layer in range(gradient.shape[1])
    ]
    for copy in copies:
        copy.start()
    for copy in copies:
        copy.wait()


def on_device(object_slices, positions, intensities, probe, propagator):
    count, width = intensities.shape[2], intensities.shape[-1]
    layers, tall, broad = object_slices.shape[1:]
    rounds = broad // LANES + 1
    tables = jnp.asarray(half_tables(width))
    anywhere = pl.BlockSpec(memory_space=pl.ANY)
    f32 = functools.partial(pltpu.VMEM, dtype=jnp.float32)
    strip, side, corner = (layers, 2, 2, 2, HALO, LANES), (layers, 2, tall, LANES), (layers, 2, 2, HALO, LANES)
    dma = pltpu.SemaphoreType.DMA
    held = pltpu.VMEM(object_slices.shape, object_slices.dtype)
    pair = [held, held]
    found = pl.pallas_call(
        step_kernel,
        out_shape=pair,
        in_specs=[anywhere] * 6,
        out_specs=[pl.BlockSpec(memory_space=pltpu.VMEM)] * 2,
        scratch_shapes=[
            pltpu.SMEM(positions.shape, positions.dtype),
            pltpu.VMEM(tables.shape, tables.dtype),
            f32(object_slices.shape),
            f32((count, width, width)),
            f32((count, width, width)),
            f32((width, width)),
            f32((2, width, width)),
            f32((count, layers, 2, width, width)),
            f32((count, layers, 2, width, width)),
            f32((2, rounds, (tall + 2 * HALO) // 8, 8, LANES)),
            f32((count, 2, rounds, (width + 4 * HALO) // 8 + 1, 8, LANES)),
            f32(strip), f32(strip), f32(side), f32(side), f32(corner),
            f32(strip), f32(strip), f32(side), f32(side), f32(corner), f32(corner),
            dma((4 + count,)), dma((layers,)),
            dma((2, layers, 2, 2)), dma((2, layers, 2)), dma((2, layers, 2)),
            dma((2, layers, 2, 2)), dma((2, layers, 2)), dma((2, layers, 2)),
        ],
        compiler_params=pltpu.CompilerParams(collective_id=0, has_side_effects=True, vmem_limit_bytes=54 * 2**20),
    )(positions, object_slices, intensities.reshape(count, width, width), probe, propagator, tables)
    like = jax.ShapeDtypeStruct(object_slices.shape, object_slices.dtype)
    return tuple(
        pl.pallas_call(
            publish_kernel,
            out_shape=[like, like],
            in_specs=[pl.BlockSpec(memory_space=pltpu.VMEM)] * 2,
            out_specs=[anywhere] * 2,
            scratch_shapes=[dma((2, layers))],
            compiler_params=pltpu.CompilerParams(vmem_limit_bytes=2**20),
        )(*(pltpu.with_memory_space_constraint(v, pltpu.VMEM) for v in found))
    )


def solution(mesh):
    return jax.shard_map(
        on_device,
        mesh=mesh,
        in_specs=(
            P(None, None, "row", "col"),
            P("row", "col", None, None),
            P("row", "col", None, None, None),
            P(),
            P(),
        ),
        out_specs=(P(None, None, "row", "col"), P(None, None, "row", "col")),
        check_vma=False,
    )
```

```python
import functools

import jax
import jax.numpy as jnp
import numpy as np
from jax import lax
from jax.experimental import pallas as pl
from jax.experimental.pallas import tpu as pltpu
from jax.sharding import PartitionSpec as P

HALO = 64
LANES = 128

descent_rate = 0.5


def split(value):
    high = value.astype(jnp.bfloat16)
    low = (value - high.astype(jnp.float32)).astype(jnp.bfloat16)
    return high, low


def half_tables(width):
    half = width // 2
    place = np.arange(half)
    found = []
    for odd in (0, 1):
        angle = 2.0 * np.pi * (np.outer(2 * place + odd, place) % width) / width
        re = np.cos(angle) / np.sqrt(width)
        im = -np.sin(angle) / np.sqrt(width)
        found.append(np.block([[re, -im], [im, re]]).astype(np.float32))
    even, odd = found
    order = np.eye(width, dtype=np.float32)[np.concatenate([2 * place, 2 * place + 1])]
    six = np.stack([even, odd, even.T, odd.T, order, order.T])
    high = six.astype(jnp.bfloat16)
    low = (six - high.astype(np.float32)).astype(jnp.bfloat16)
    return np.stack([high, low])


def dot_left(pair, value):
    high, low = split(value)
    matrix = jnp.concatenate([pair[0], pair[0], pair[1]], 1)
    return jnp.dot(matrix, jnp.concatenate([high, low, high], 0), preferred_element_type=jnp.float32)


def dot_right(value, pair):
    high, low = split(value)
    matrix = jnp.concatenate([pair[0], pair[0], pair[1]], 0)
    return jnp.dot(jnp.concatenate([high, low, high], 1), matrix, preferred_element_type=jnp.float32)


def cut(value, dim):
    half = value.shape[dim] // 2
    return (lax.slice_in_dim(value, 0, half, axis=dim), lax.slice_in_dim(value, half, 2 * half, axis=dim))


def joined(first, second, dim):
    return jnp.concatenate([first, second], dim)


def forward_axis(re, im, dim, dot, even_matrix, odd_matrix):
    r0, r1 = cut(re, dim)
    i0, i1 = cut(im, dim)
    even_re, even_im = cut(dot(joined(r0 + r1, i0 + i1, dim), even_matrix), dim)
    odd_re, odd_im = cut(dot(joined(r0 - r1, i0 - i1, dim), odd_matrix), dim)
    return joined(even_re, odd_re, dim), joined(even_im, odd_im, dim)


def inverse_axis(re, im, dim, dot, even_matrix, odd_matrix):
    r0, r1 = cut(re, dim)
    i0, i1 = cut(im, dim)
    p_re, p_im = cut(dot(joined(r0, i0, dim), even_matrix), dim)
    q_re, q_im = cut(dot(joined(r1, i1, dim), odd_matrix), dim)
    return joined(p_re + q_re, p_re - q_re, dim), joined(p_im + q_im, p_im - q_im, dim)


def left_dot(value, pair):
    return dot_left(pair, value)


def turned_over(value, width, source, target):
    parts = [lax.slice_in_dim(value, at, at + width, axis=source) for at in range(0, value.shape[source], width)]
    return jnp.concatenate(parts, target)


def forward(re, im, pairs):
    width = re.shape[0]
    re, im = forward_axis(re, im, 0, left_dot, pairs(0), pairs(1))
    re, im = (turned_over(v, width, 1, 0) for v in (re, im))
    return forward_axis(re, im, 1, dot_right, pairs(2), pairs(3))


def inverse(re, im, pairs):
    width = re.shape[1]
    re, im = inverse_axis(re, im, 1, dot_right, pairs(0), pairs(1))
    re, im = (turned_over(v, width, 0, 1) for v in (re, im))
    return inverse_axis(re, im, 0, left_dot, pairs(2), pairs(3))


def hop(fields, phase_re, phase_im, pairs):
    width = fields[0][0].shape[0]
    re, im = forward(*(jnp.concatenate([f[c] for f in fields], 1) for c in range(2)), pairs)
    re, im = complex_product(re, im, *(jnp.concatenate([p] * len(fields), 0) for p in (phase_re, phase_im)))
    re, im = inverse(re, im, pairs)
    spans = [slice(at, at + width) for at in range(0, re.shape[1], width)]
    return [(re[:, span], im[:, span]) for span in spans]


def by_parity(value, left, right):
    rows = jnp.dot(
        jnp.concatenate([left, left], 1), jnp.concatenate(split(value), 0), preferred_element_type=jnp.float32
    )
    return jnp.dot(
        jnp.concatenate(split(rows), 1), jnp.concatenate([right, right], 0), preferred_element_type=jnp.float32
    )


def complex_product(left_re, left_im, right_re, right_im):
    return (left_re * right_re - left_im * right_im, left_re * right_im + left_im * right_re)


def slid(whole, shift, axis, span):
    turned = pltpu.roll(whole, lax.rem(span - shift, span), axis)
    kept = lax.broadcasted_iota(jnp.int32, whole[:-1].shape, axis) < span - shift
    return jnp.where(kept, turned[:-1], turned[1:])


def spread(whole, shift, axis, span):
    turned = pltpu.roll(whole, lax.rem(shift, span), axis)
    zero = jnp.zeros_like(turned[:1])
    first = jnp.concatenate([zero, turned], 0)
    other = jnp.concatenate([turned, zero], 0)
    moved = lax.broadcasted_iota(jnp.int32, first.shape, axis) < shift
    return jnp.where(moved, first, other)


def row_place(oy, rows, width):
    base = jnp.minimum(lax.div(oy, 8), (rows - width) // 8 - 1)
    return base, oy - 8 * base


def lane_place(ox):
    early = ox < HALO
    return jnp.where(early, 2, 0), jnp.where(early, ox + LANES - HALO, ox - HALO)


def swapped(value):
    return pltpu.roll(value, HALO, value.ndim - 1)


def choose(low, high):
    lower = lax.broadcasted_iota(jnp.int32, low.shape, low.ndim - 1) < HALO
    return jnp.where(lower, low, high)


def ends_of(cells):
    (re0, re1), (im0, im1) = cells
    return choose(re0, swapped(im0)), choose(swapped(re1), im1)


def middle_of(cells):
    return [choose(swapped(first), swapped(second)) for first, second in cells]


def unpacked(head, tail, middle_re, middle_im):
    mid_re, mid_im = swapped(middle_re), swapped(middle_im)
    return (
        (choose(head, mid_re), choose(mid_re, swapped(tail))),
        (choose(swapped(head), mid_im), choose(mid_im, tail)),
    )


def step_kernel(
    offsets_in, objects, intensities, probe, propagator, tables_in,
    gradient, updated,
    offsets, tables, cells, measured, ordered, phase, phases, waves, windows, slab, spans,
    row_out, row_in, col_out, col_in, corner_in,
    grow_out, grow_in, gcol_out, gcol_in, gcorner_out, gcorner_in,
    load_sem, slice_sem, row_sem, col_sem, corner_sem, grow_sem, gcol_sem, gcorner_sem,
):
    count, width = measured.shape[0], measured.shape[-1]
    layers, tall = cells.shape[1:3]
    last = layers - 1
    wide = cells.shape[3] // LANES
    rounds = wide + 1
    whole = tall + 2 * HALO
    pad = 2 * HALO

    rows_n, cols_n = lax.axis_size("row"), lax.axis_size("col")
    row, col = lax.axis_index("row"), lax.axis_index("col")
    below, above = lax.rem(row + 1, rows_n), lax.rem(row + rows_n - 1, rows_n)
    right, left = lax.rem(col + 1, cols_n), lax.rem(col + cols_n - 1, cols_n)
    row_to = ((below, col), (above, col))
    col_to = ((row, right), (row, left))

    def send(src, dst, sems, where, target):
        return pltpu.make_async_remote_copy(
            src_ref=src, dst_ref=dst, send_sem=sems.at[(0, *where)], recv_sem=sems.at[(1, *where)],
            device_id=target, device_id_type=pl.DeviceIdType.MESH,
        )

    def row_copy(layer, half, d):
        where = (layer, half, slice(None), d)
        target = (lax.rem(row + rows_n + 1 - 2 * d, rows_n), col)
        return send(row_out.at[where], row_in.at[where], row_sem, (layer, half, d), target)

    def col_copy(layer, side):
        return send(col_out.at[layer, side], col_in.at[layer, side], col_sem, (layer, side), col_to[side])

    def corner_copy(layer, side):
        source = row_in.at[layer, 0, 1 - side]
        return send(source, corner_in.at[layer, side], corner_sem, (layer, side), col_to[side])

    def grow_copy(layer, half, d):
        where = (layer, half, slice(None), d)
        target = (lax.rem(row + rows_n + 1 - 2 * d, rows_n), col)
        return send(grow_out.at[where], grow_in.at[where], grow_sem, (layer, half, d), target)

    def gcol_copy(layer, side):
        return send(gcol_out.at[layer, side], gcol_in.at[layer, side], gcol_sem, (layer, side), col_to[side])

    def gcorner_copy(layer, side):
        return send(
            gcorner_out.at[layer, side], gcorner_in.at[layer, side], gcorner_sem, (layer, side), col_to[side]
        )

    loads = [
        pltpu.make_async_copy(propagator, phase, load_sem.at[0]),
        pltpu.make_async_copy(tables_in, tables, load_sem.at[1]),
        pltpu.make_async_copy(intensities, measured, load_sem.at[2]),
        pltpu.make_async_copy(offsets_in, offsets, load_sem.at[3]),
    ] + [pltpu.make_async_copy(probe, waves.at[k, 0], load_sem.at[4 + k]) for k in range(count)]

    def slice_load(layer):
        return pltpu.make_async_copy(objects.at[:, layer], cells.at[:, layer], slice_sem.at[layer])

    barrier = pltpu.get_barrier_semaphore()
    for target in row_to + col_to:
        pl.semaphore_signal(barrier, inc=1, device_id=target, device_id_type=pl.DeviceIdType.MESH)
    for layer in range(layers):
        slice_load(layer).start()

    def lane_blocks(ref, layer, rows):
        return [[ref[c, layer, rows, pl.ds(j * LANES, LANES)] for j in range(wide)] for c in range(2)]

    def pack(layer):
        slice_load(layer).wait()
        for d, at in enumerate((tall - HALO, 0)):
            strip = lane_blocks(cells, layer, pl.ds(at, HALO))
            for half, packs in enumerate((ends_of(strip), middle_of(strip))):
                for i in range(2):
                    row_out[layer, half, i, d] = packs[i]

    def pack_sides(layer):
        head, tail = ends_of(lane_blocks(cells, layer, pl.ds(0, tall)))
        col_out[layer, 0] = tail
        col_out[layer, 1] = head

    def launch(layer):
        for d in range(2):
            for half in range(2):
                row_copy(layer, half, d).start()

    def pack_and_launch(layer, carry):
        pack(layer)
        launch(layer)
        pack_sides(layer)
        launch_sides(layer)
        return carry

    def launch_sides(layer):
        for side in range(2):
            col_copy(layer, side).start()

    pack(0)
    pl.semaphore_wait(barrier, 4)
    launch(0)
    pack_sides(0)
    launch_sides(0)
    for load in loads:
        load.start()
    lax.fori_loop(1, layers, pack_and_launch, 0)

    def pairs(index):
        return tables[0, index], tables[1, index]

    for load in loads:
        load.wait()
    angle = phase[...]
    phases[0] = by_parity(jnp.cos(angle), tables[0, 4], tables[0, 5])
    phases[1] = by_parity(jnp.sin(angle), tables[0, 4], tables[0, 5])
    for k in range(count):
        ordered[k] = by_parity(measured[k], tables[0, 4], tables[0, 5])
    blank = jnp.zeros((pad // 8, 8, LANES), jnp.float32)
    for k in range(count):
        for c in range(2):
            for j in range(rounds):
                spans[k, c, j, pl.ds(0, pad // 8)] = blank
                spans[k, c, j, pl.ds((pad + width) // 8 + 1, pad // 8)] = blank

    def forward_corners(layer):
        for d in range(2):
            row_copy(layer, 0, d).wait_recv()
        for side in range(2):
            corner_copy(layer, side).start()

    def assemble(layer):
        def place(start, size, blocks, l, r):
            rows, tiles = pl.ds(start // 8, size // 8), (size // 8, 8, LANES)
            for c in range(2):
                for j in range(wide):
                    slab[c, j, rows] = blocks[c][j].reshape(tiles)
            slab[0, wide, rows] = choose(r, swapped(l)).reshape(tiles)
            slab[1, wide, rows] = choose(swapped(r), l).reshape(tiles)

        for side in range(2):
            col_copy(layer, side).wait_recv()
        place(HALO, tall, lane_blocks(cells, layer, pl.ds(0, tall)), col_in[layer, 0], col_in[layer, 1])
        for d in range(2):
            row_copy(layer, 1, d).wait_recv()
        for side in range(2):
            corner_copy(layer, side).wait_recv()
        for d, start in enumerate((0, HALO + tall)):
            blocks = unpacked(*(row_in[layer, half, i, d] for half in range(2) for i in range(2)))
            place(start, HALO, blocks, corner_in[layer, 0, d], corner_in[layer, 1, d])

    def cut_layer(k, layer):
        base, shift = row_place(offsets[0, 0, k, 0], whole, width)
        first, turn = lane_place(offsets[0, 0, k, 1])
        for c in range(2):
            blocks = jnp.stack(
                [slab[c, lax.rem(first + j, rounds), pl.ds(base, width // 8 + 1)] for j in range(rounds)]
            )
            blocks = slid(blocks, turn, 3, LANES)
            for j in range(wide):
                part = slid(blocks[j], shift, 1, 8)
                windows[k, layer, c, :, j * LANES : j * LANES + LANES] = part.reshape(width, LANES)

    def leave(k, layer):
        return complex_product(
            waves[k, layer, 0], waves[k, layer, 1], windows[k, layer, 0], windows[k, layer, 1]
        )

    def onward(layer, carry):
        assemble(layer)
        for k in range(count):
            cut_layer(k, layer)
            if k == 0:
                forward_corners(layer + 1)
            ((re, im),) = hop([leave(k, layer)], phases[0], phases[1], pairs)
            waves[k, layer + 1, 0] = re
            waves[k, layer + 1, 1] = im
        return carry

    forward_corners(0)
    lax.fori_loop(0, last, onward, 0)

    def record(k, layer, back_re, back_im, start, stop):
        low, high = max(start - 1, 0), min(stop, width // 8)
        rows, span = pl.ds(8 * low, 8 * (high - low)), slice(8 * low, 8 * high)
        wave_re, wave_im = waves[k, layer, 0, rows, :], waves[k, layer, 1, rows, :]
        back_re, back_im = back_re[span], back_im[span]
        shift = row_place(offsets[0, 0, k, 0], whole, width)[1]
        turn = lane_place(offsets[0, 0, k, 1])[1]
        terms = (wave_re * back_re + wave_im * back_im, wave_re * back_im - wave_im * back_re)
        for c in range(2):
            blocks = jnp.stack([terms[c][:, j * LANES : j * LANES + LANES] for j in range(wide)])
            blocks = spread(blocks, turn, 2, LANES)
            for j in range(rounds):
                turned = pltpu.roll(blocks[j].reshape(high - low, 8, LANES), lax.rem(shift, 8), 1)
                zero = jnp.zeros_like(turned[:1])
                before, after = turned[: stop - 1 - low], turned[start - low :]
                if start == 0:
                    before = jnp.concatenate([zero, before], 0)
                if stop > high:
                    after = jnp.concatenate([after, zero], 0)
                else:
                    after = after[: stop - start]
                moved = lax.broadcasted_iota(jnp.int32, before.shape, 1) < shift
                spans[k, c, j, pl.ds(pad // 8 + start, stop - start)] = jnp.where(moved, before, after)

    def summed(c, block, start, size):
        found = None
        for k in range(count):
            base = row_place(offsets[0, 0, k, 0], whole, width)[0]
            first = lane_place(offsets[0, 0, k, 1])[0]
            at = (pad + start) // 8 - base
            term = spans[k, c, lax.rem(block + rounds - first, rounds), pl.ds(at, size // 8)]
            found = term if found is None else found + term
        return found.reshape(size, LANES)

    def sums(start, size):
        blocks = [[summed(c, j, start, size) for j in range(wide)] for c in range(2)]
        outer_re, outer_im = (summed(c, wide, start, size) for c in range(2))
        return blocks, (choose(outer_re, swapped(outer_im)), choose(swapped(outer_re), outer_im))

    def settle(layer, backs):
        reach = HALO // 8
        for k in range(count):
            record(k, layer, *backs[k], 0, reach)
            record(k, layer, *backs[k], width // 8 + 1 - reach, width // 8 + 1)
        for d, start in enumerate((0, HALO + tall)):
            blocks, outer = sums(start, HALO)
            for half, packs in enumerate((ends_of(blocks), middle_of(blocks))):
                for i in range(2):
                    grow_out[layer, half, i, 1 - d] = packs[i]
            for side in range(2):
                gcorner_out[layer, side, 1 - d] = outer[side]
        for d in range(2):
            grow_copy(layer, 1, d).start()
        for side in range(2):
            gcorner_copy(layer, side).start()
        for k in range(count):
            record(k, layer, *backs[k], reach, width // 8 + 1 - reach)
        blocks, outer = sums(HALO, tall)
        for c in range(2):
            for j in range(wide):
                gradient[c, layer, :, j * LANES : j * LANES + LANES] = blocks[c][j]
        for side in range(2):
            gcol_out[layer, side] = outer[side]
            gcol_copy(layer, side).start()
        for k in range(count):
            for c in range(2):
                waves[k, layer, c] = backs[k][c]

    def pass_on(layer):
        for side in range(2):
            gcorner_copy(layer, side).wait_recv()
        for d in range(2):
            for side in range(2):
                grow_out[layer, 0, side, d] += gcorner_in[layer, side, d]
        for d in range(2):
            grow_copy(layer, 0, d).start()

    assemble(last)
    for k in range(count):
        cut_layer(k, last)
    leaving = [leave(k, last) for k in range(count)]
    far_re, far_im = forward(*(jnp.concatenate([v[c] for v in leaving], 1) for c in range(2)), pairs)
    misfit = far_re * far_re + far_im * far_im - ordered[...].reshape(far_re.shape)
    backs = inverse(misfit * far_re, misfit * far_im, pairs)
    settle(last, [[v[:, k * width : (k + 1) * width] for v in backs] for k in range(count)])

    def backward(step, carry):
        layer = last - step
        fields = []
        for k in range(count):
            back_re, back_im = waves[k, layer, 0], waves[k, layer, 1]
            slab_re, slab_im = windows[k, layer, 0], windows[k, layer, 1]
            fields.append(complex_product(back_re, back_im, slab_re, -slab_im))
        backs = hop(fields, phases[0], -phases[1], pairs)
        pass_on(layer)
        settle(layer - 1, backs)
        return carry

    lax.fori_loop(0, last, backward, 0)
    pass_on(0)
    def close_in(layer, carry):
        for d in range(2):
            for half in range(2):
                row_copy(layer, half, d).wait_send()
            col_copy(layer, d).wait_send()
            corner_copy(layer, d).wait_send()
        return carry

    lax.fori_loop(0, layers, close_in, 0)

    def finish(step, carry):
        layer = last - step
        for side in range(2):
            gcol_copy(layer, side).wait_recv()
        spots = ((HALO, tall - 2 * HALO, None), (0, HALO, 0), (tall - HALO, HALO, 1))
        for start, size, d in spots:
            if d == 0:
                for half in (1, 0):
                    for e in range(2):
                        grow_copy(layer, half, e).wait_recv()
            rows = pl.ds(start, size)
            sums = lane_blocks(gradient, layer, rows)
            if d is not None:
                added = unpacked(*(grow_in[layer, half, i, d] for half in range(2) for i in range(2)))
                sums = [[sums[c][j] + added[c][j] for j in range(wide)] for c in range(2)]
            l, r = gcol_in[layer, 0, rows, :], gcol_in[layer, 1, rows, :]
            zero = jnp.zeros_like(l)
            sums[0][0] += choose(l, zero)
            sums[1][0] += choose(swapped(l), zero)
            sums[0][wide - 1] += choose(zero, swapped(r))
            sums[1][wide - 1] += choose(zero, r)
            for c in range(2):
                for j in range(wide):
                    lanes = pl.ds(j * LANES, LANES)
                    gradient[c, layer, rows, lanes] = sums[c][j]
                    updated[c, layer, rows, lanes] = cells[c, layer, rows, lanes] - descent_rate * sums[c][j]
        return carry

    lax.fori_loop(0, layers, finish, 0)

    def close_out(layer, carry):
        for d in range(2):
            for half in range(2):
                grow_copy(layer, half, d).wait_send()
            gcol_copy(layer, d).wait_send()
            gcorner_copy(layer, d).wait_send()
        return carry

    lax.fori_loop(0, layers, close_out, 0)


def publish_kernel(gradient, updated, gradient_out, updated_out, sems):
    copies = [
        pltpu.make_async_copy(held.at[:, layer], out.at[:, layer], sems.at[i, layer])
        for i, (held, out) in enumerate(((gradient, gradient_out), (updated, updated_out)))
        for layer in range(gradient.shape[1])
    ]
    for copy in copies:
        copy.start()
    for copy in copies:
        copy.wait()


def on_device(object_slices, positions, intensities, probe, propagator):
    count, width = intensities.shape[2], intensities.shape[-1]
    layers, tall, broad = object_slices.shape[1:]
    rounds = broad // LANES + 1
    tables = jnp.asarray(half_tables(width))
    anywhere = pl.BlockSpec(memory_space=pl.ANY)
    f32 = functools.partial(pltpu.VMEM, dtype=jnp.float32)
    strip, side, corner = (layers, 2, 2, 2, HALO, LANES), (layers, 2, tall, LANES), (layers, 2, 2, HALO, LANES)
    dma = pltpu.SemaphoreType.DMA
    held = pltpu.VMEM(object_slices.shape, object_slices.dtype)
    pair = [held, held]
    found = pl.pallas_call(
        step_kernel,
        out_shape=pair,
        in_specs=[anywhere] * 6,
        out_specs=[pl.BlockSpec(memory_space=pltpu.VMEM)] * 2,
        scratch_shapes=[
            pltpu.SMEM(positions.shape, positions.dtype),
            pltpu.VMEM(tables.shape, tables.dtype),
            f32(object_slices.shape),
            f32((count, width, width)),
            f32((count, width, width)),
            f32((width, width)),
            f32((2, width, width)),
            f32((count, layers, 2, width, width)),
            f32((count, layers, 2, width, width)),
            f32((2, rounds, (tall + 2 * HALO) // 8, 8, LANES)),
            f32((count, 2, rounds, (width + 4 * HALO) // 8 + 1, 8, LANES)),
            f32(strip), f32(strip), f32(side), f32(side), f32(corner),
            f32(strip), f32(strip), f32(side), f32(side), f32(corner), f32(corner),
            dma((4 + count,)), dma((layers,)),
            dma((2, layers, 2, 2)), dma((2, layers, 2)), dma((2, layers, 2)),
            dma((2, layers, 2, 2)), dma((2, layers, 2)), dma((2, layers, 2)),
        ],
        compiler_params=pltpu.CompilerParams(collective_id=0, has_side_effects=True, vmem_limit_bytes=54 * 2**20),
    )(positions, object_slices, intensities.reshape(count, width, width), probe, propagator, tables)
    like = jax.ShapeDtypeStruct(object_slices.shape, object_slices.dtype)
    return tuple(
        pl.pallas_call(
            publish_kernel,
            out_shape=[like, like],
            in_specs=[pl.BlockSpec(memory_space=pltpu.VMEM)] * 2,
            out_specs=[anywhere] * 2,
            scratch_shapes=[dma((2, layers))],
            compiler_params=pltpu.CompilerParams(vmem_limit_bytes=2**20),
        )(*(pltpu.with_memory_space_constraint(v, pltpu.VMEM) for v in found))
    )


def solution(mesh):
    return jax.shard_map(
        on_device,
        mesh=mesh,
        in_specs=(
            P(None, None, "row", "col"),
            P("row", "col", None, None),
            P("row", "col", None, None, None),
            P(),
            P(),
        ),
        out_specs=(P(None, None, "row", "col"), P(None, None, "row", "col")),
        check_vma=False,
    )
```
